512 devices in a mesh: seq: 128 (over z, y, core), tp: 4 (over x).
Axes of the slice: x: 4, y: 8, z: 8, core: 2. Of those that a mesh axis runs over, the one named last changes fastest.
Arguments:
- queries: bfloat16 [4096, 1536], P('seq', 'tp'), may hold values from -100 to 100
- new_keys: bfloat16 [4096, 1536], P('seq', 'tp'), may hold values from -16 to 16
- new_values: bfloat16 [4096, 1536], P('seq', 'tp'), may hold values from -6 to 6
- forget_logit: float32 [24, 4096], P('tp', 'seq'), may hold values from 0 to 20
- cache_keys: bfloat16 [262144, 1536], P('seq', 'tp'), may hold values from -16 to 16
- cache_values: bfloat16 [262144, 1536], P('seq', 'tp'), may hold values from -6 to 6
- cache_decay: float32 [24, 262144], P('tp', 'seq'), may hold values from 0 to 32768, as said below
- slot_page: int32 [2048], P('seq'), may hold values from 0 to 255, as said below
- cache_len: int32 [8], replicated, may hold values from 1 to 32768, as said below
- residual: bfloat16 [4096, 1536], P('seq', 'tp'), may hold values from -6 to 6
- out_weight: bfloat16 [1536, 1536], P('tp'), may hold values from -0.15625 to 0.15625
Outputs:
- layer_out: bfloat16 [4096, 1536], P('seq', 'tp')
- new_forget: float32 [24, 4096], P('tp', 'seq')
The draws below stay inside these ranges and needn't reach their ends.
Inputs may be any that keep to these rules, and one draw needn't show every extreme that they name: `slot_page`: within the slots of each request, every page number 0 to 255 stands exactly once. `cache_len`: some request has exactly 32768 cached tokens. `cache_decay`: over the live slots of one request and one head it does not rise as the position rises.
All inputs are finite; a program needn't handle non-finite values.
Results may differ from the reference program's by a relative error of at most 0.0075.
Values may be sent and summed in bfloat16 or wider, within the bound.
A program may use at most 64 MiB of HBM per device.

```python
import jax
import jax.numpy as jnp
from jax import lax

D = 1536
HEAD_TOTAL = 24
HEAD_DIM = 64
REQUEST_TOTAL = 8
PAGE = 128
NEW = 512
TOKEN_TOTAL = 4096
MAX_SLOT_LENGTH = 32768
SLOTS = 262144


def request_layout(key):
    lengths = jax.random.randint(jax.random.fold_in(key, 7), (REQUEST_TOTAL,), 1, MAX_SLOT_LENGTH + 1)
    longest = jax.random.randint(jax.random.fold_in(key, 8), (), 0, REQUEST_TOTAL)
    lengths = jnp.where(jnp.arange(REQUEST_TOTAL) == longest, MAX_SLOT_LENGTH, lengths).astype(jnp.int32)
    page_keys = jax.random.split(jax.random.fold_in(key, 9), REQUEST_TOTAL)
    pages = jax.vmap(lambda single: jax.random.permutation(single, MAX_SLOT_LENGTH // PAGE))(page_keys)
    return (lengths, pages.reshape(-1).astype(jnp.int32))


def head_rates(key):
    picked = jax.random.uniform(jax.random.fold_in(key, 21), (REQUEST_TOTAL, HEAD_TOTAL))
    rapid = jax.random.uniform(jax.random.fold_in(key, 22), (REQUEST_TOTAL, HEAD_TOTAL), minval=1.0 / 50.0, maxval=1.0 / 30.0)
    lasting = jnp.exp(jax.random.uniform(jax.random.fold_in(key, 23), (REQUEST_TOTAL, HEAD_TOTAL), minval=jnp.log(0.05 / MAX_SLOT_LENGTH), maxval=jnp.log(2.0 / MAX_SLOT_LENGTH)))
    share = 0.5
    return jnp.where(picked < share, rapid, lasting)


def drawn_keys(key):
    base_rows = jax.random.truncated_normal(jax.random.fold_in(key, 51), -5.0, 5.0, (TOKEN_TOTAL, D))
    key_rows = base_rows
    return key_rows


def draw_cache_len(key, part):
    lengths, pages = request_layout(key)
    return lengths


def draw_slot_page(key, part):
    lengths, pages = request_layout(key)
    return pages


def draw_cache_decay(key, part):
    lengths, pages = request_layout(key)
    rates = head_rates(key)
    slot_index = jnp.arange(SLOTS)
    owning_request = slot_index // MAX_SLOT_LENGTH
    token_positions = pages[slot_index // PAGE] * PAGE + slot_index % PAGE
    request_length = lengths[owning_request]
    rate_rows = rates[owning_request].T
    decay_factor = rate_rows * (request_length - 1 - token_positions).astype(jnp.float32)[None, :]
    for spike_event in range(3):
        spike_position = jax.random.randint(jax.random.fold_in(key, 31 + spike_event), (HEAD_TOTAL, REQUEST_TOTAL), 0, MAX_SLOT_LENGTH)[:, owning_request]
        spike_length = jax.random.uniform(jax.random.fold_in(key, 41 + spike_event), (HEAD_TOTAL, REQUEST_TOTAL), minval=0.22, maxval=0.69)[:, owning_request]
        placed_slots = (spike_position > token_positions[None, :]) & (spike_position < request_length[None, :])
        decay_factor = decay_factor + jnp.where(placed_slots, spike_length, 0.0)
    filler = jax.random.uniform(jax.random.fold_in(key, 49), (HEAD_TOTAL, SLOTS))
    return jnp.where((token_positions < request_length)[None, :], decay_factor, filler).astype(jnp.float32)


def draw_forget_logit(key, part):
    rates = head_rates(key)
    owning_request = jnp.arange(TOKEN_TOTAL) // NEW
    middle_point = -jnp.log(rates[owning_request].T)
    random_offset = jax.random.uniform(jax.random.fold_in(key, 61), (HEAD_TOTAL, TOKEN_TOTAL), minval=-0.7, maxval=0.7)
    spiky_lengths = jax.random.uniform(jax.random.fold_in(key, 62), (HEAD_TOTAL, TOKEN_TOTAL)) < 1.0 / 128.0
    spike_value = jax.random.uniform(jax.random.fold_in(key, 63), (HEAD_TOTAL, TOKEN_TOTAL), minval=0.0, maxval=1.4)
    return jnp.where(spiky_lengths, spike_value, middle_point + random_offset).astype(jnp.float32)


def draw_new_keys(key, part):
    key_rows = drawn_keys(key)
    return key_rows.astype(jnp.bfloat16)


def draw_queries(key, part):
    base_rows = jax.random.truncated_normal(jax.random.fold_in(key, 52), -5.0, 5.0, (TOKEN_TOTAL, D))
    rows_out = base_rows
    return rows_out.astype(jnp.bfloat16)


def draw_cache_keys(key, part):
    slot_rows = jax.random.truncated_normal(jax.random.fold_in(key, 71), -6.0, 6.0, (SLOTS, D))
    return slot_rows.astype(jnp.bfloat16)


def block_scale(stream_key, extent, shards, least, largest):
    loudness = 1.0
    for dim, blocks in shards:
        steps = jax.random.uniform(jax.random.fold_in(jax.random.fold_in(stream_key, 6), dim), (blocks,), jnp.float32, least / len(shards), largest / len(shards))
        loudness = loudness * jnp.repeat(jnp.exp(steps), extent[dim] // blocks).reshape((-1,) + (1,) * (len(extent) - 1 - dim))
    return loudness


def bell_draw(rng, extent, spread, most, pieces=(), kind=jnp.bfloat16):
    factor_of = block_scale(rng, extent, pieces, -0.22, 0.18) if pieces else 1.0
    array = jax.random.normal(rng, extent, jnp.float32) * spread * factor_of
    return jnp.minimum(jnp.maximum(array, -most), most).astype(kind)


def setup_inputs(seed: int = 0) -> dict:
    key_of = jax.random.split(jax.random.key(seed), 12)
    return {
        "queries": draw_queries(jax.random.fold_in(key_of[11], 71), 0),
        "new_keys": draw_new_keys(jax.random.fold_in(key_of[11], 71), 0),
        "new_values": bell_draw(key_of[2], (TOKEN_TOTAL, D), 1.0, 6.0, ((0, 128), (1, 4))),
        "forget_logit": draw_forget_logit(jax.random.fold_in(key_of[11], 71), 0),
        "cache_keys": draw_cache_keys(jax.random.fold_in(key_of[11], 71), 0),
        "cache_values": bell_draw(key_of[5], (SLOTS, D), 1.0, 6.0, ((0, 128), (1, 4))),
        "cache_decay": draw_cache_decay(jax.random.fold_in(key_of[11], 71), 0),
        "slot_page": draw_slot_page(jax.random.fold_in(key_of[11], 71), 0),
        "cache_len": draw_cache_len(jax.random.fold_in(key_of[11], 71), 0),
        "residual": bell_draw(key_of[9], (TOKEN_TOTAL, D), 1.0, 6.0, ((0, 128), (1, 4))),
        "out_weight": bell_draw(key_of[10], (D, D), D ** -0.5, 0.15625, ((0, 4),)),
    }


def reference(queries, new_keys, new_values, forget_logit, cache_keys, cache_values, cache_decay, slot_page, cache_len, residual, out_weight):
    scale = HEAD_DIM ** -0.5
    log_forget = jax.nn.log_sigmoid(forget_logit)
    new_forget = jnp.cumsum(log_forget.reshape(HEAD_TOTAL, REQUEST_TOTAL, NEW), axis=2).reshape(HEAD_TOTAL, TOKEN_TOTAL)
    key_span = min(2048, MAX_SLOT_LENGTH)
    span_count = MAX_SLOT_LENGTH // key_span
    page_count = MAX_SLOT_LENGTH // PAGE
    query_index = jnp.arange(NEW, dtype=jnp.int32)
    causal = query_index[None, :] <= query_index[:, None]

    def one_request(request):
        first_row = request * NEW
        first_slot = request * MAX_SLOT_LENGTH
        query_heads = lax.dynamic_slice_in_dim(queries, first_row, NEW, 0).astype(jnp.float32).reshape(NEW, HEAD_TOTAL, HEAD_DIM)
        fresh_keys = lax.dynamic_slice_in_dim(new_keys, first_row, NEW, 0).reshape(NEW, HEAD_TOTAL, HEAD_DIM)
        fresh_values = lax.dynamic_slice_in_dim(new_values, first_row, NEW, 0).reshape(NEW, HEAD_TOTAL, HEAD_DIM)
        query_forget = lax.dynamic_slice_in_dim(new_forget, first_row, NEW, 1)
        forget_rows = query_forget.T
        pages = lax.dynamic_slice_in_dim(slot_page, request * page_count, page_count, 0)
        token_positions = (pages[:, None] * PAGE + jnp.arange(PAGE, dtype=jnp.int32)[None, :]).reshape(MAX_SLOT_LENGTH)
        request_length = lax.dynamic_slice_in_dim(cache_len, request, 1, 0)[0]
        alive = (token_positions < request_length).reshape(span_count, 1, key_span)
        key_blocks = lax.dynamic_slice_in_dim(cache_keys, first_slot, MAX_SLOT_LENGTH, 0).reshape(span_count, key_span, HEAD_TOTAL, HEAD_DIM)
        value_blocks = lax.dynamic_slice_in_dim(cache_values, first_slot, MAX_SLOT_LENGTH, 0).reshape(span_count, key_span, HEAD_TOTAL, HEAD_DIM)
        decay_blocks = lax.dynamic_slice_in_dim(cache_decay, first_slot, MAX_SLOT_LENGTH, 1).reshape(HEAD_TOTAL, span_count, key_span).transpose(1, 0, 2)

        def scores_of(key_rows, key_decay, key_mask):
            raw = jnp.einsum("ihd,khd->ihk", query_heads, key_rows.astype(jnp.float32))
            scored = raw * scale + forget_rows[:, :, None] - key_decay[None, :, :]
            return jnp.where(key_mask[:, None, :], scored, -jnp.inf)

        fresh_scores = scores_of(fresh_keys, query_forget, causal)

        def max_step(highest, segment):
            key_rows, value_rows, key_decay, key_mask = segment
            return jnp.maximum(highest, jnp.max(scores_of(key_rows, key_decay, key_mask), axis=2)), None

        highest, _ = lax.scan(max_step, jnp.max(fresh_scores, axis=2), (key_blocks, value_blocks, decay_blocks, alive))

        def weigh(scored, value_rows):
            exps = jnp.exp(scored - highest[:, :, None])
            rounded = lax.optimization_barrier(exps.astype(jnp.bfloat16)).astype(jnp.float32)
            return jnp.sum(exps, axis=2), jnp.einsum("ihk,khd->ihd", rounded, value_rows.astype(jnp.float32))

        def sum_step(carry, segment):
            key_rows, value_rows, key_decay, key_mask = segment
            denominator, weighted = weigh(scores_of(key_rows, key_decay, key_mask), value_rows)
            return (carry[0] + denominator, carry[1] + weighted), None

        totals, _ = lax.scan(sum_step, weigh(fresh_scores, fresh_values), (key_blocks, value_blocks, decay_blocks, alive))
        denominator, weighted = totals
        return (weighted / denominator[:, :, None]).reshape(NEW, D).astype(jnp.bfloat16)

    attention = lax.map(one_request, jnp.arange(REQUEST_TOTAL, dtype=jnp.int32)).reshape(TOKEN_TOTAL, D)
    projected = jnp.dot(attention, out_weight, preferred_element_type=jnp.float32)
    layer_out = (residual.astype(jnp.float32) + projected).astype(jnp.bfloat16)
    return layer_out, new_forget
```

```python
import functools

import jax
import jax.numpy as jnp
from jax import lax
from jax.experimental import pallas as pl
from jax.experimental.pallas import tpu as pltpu
from jax.sharding import PartitionSpec as P

HEAD_DIM = 64
PAGE = 128
CHIPS = 8
GROUP = 16
DEAD = 1e30
MESH = pl.DeviceIdType.MESH


def thirds(x):
    high = x.astype(jnp.bfloat16)
    rest = x - high.astype(jnp.float32)
    middle = rest.astype(jnp.bfloat16)
    low = (rest - middle.astype(jnp.float32)).astype(jnp.bfloat16)
    return high, middle, low


def layer_kernel(
    tp_count,
    q_ref,
    new_keys,
    new_values,
    logit_ref,
    cache_keys,
    cache_values,
    decay_ref,
    page_ref,
    length_ref,
    residual_ref,
    out_weight,
    out_ref,
    forget_ref,
    keys,
    values,
    weight,
    costs,
    queries,
    forget_tile,
    forget_all,
    parts_out,
    parts_in,
    shares_out,
    shares_in,
    local_sem,
    query_send,
    query_recv,
    forget_send,
    forget_recv,
    part_send,
    part_recv,
    share_send,
    share_recv,
):
    rows, width = q_ref.shape
    heads = width // HEAD_DIM
    pairs = heads // 2
    slots = cache_keys.shape[0]
    all_keys = keys.shape[0]
    seq = lax.axis_index("seq")
    tp = lax.axis_index("tp")
    request = seq // GROUP
    chip = (seq % GROUP) // 2
    core = seq % 2

    def device(chip_step, other):
        there = (chip + chip_step) % CHIPS
        return (request * GROUP + there * 2 + (1 - core if other else core), tp)

    local = [
        pltpu.make_async_copy(cache_keys, keys.at[pl.ds(0, slots)], local_sem.at[0]),
        pltpu.make_async_copy(new_keys, keys.at[pl.ds(slots, rows)], local_sem.at[1]),
        pltpu.make_async_copy(cache_values, values.at[pl.ds(0, slots)], local_sem.at[2]),
        pltpu.make_async_copy(new_values, values.at[pl.ds(slots, rows)], local_sem.at[3]),
        pltpu.make_async_copy(out_weight, weight, local_sem.at[4]),
        pltpu.make_async_copy(q_ref, queries.at[0, 0], local_sem.at[5]),
    ]
    for copy in local:
        copy.start()

    barrier = pltpu.get_barrier_semaphore()
    peers = [(step, other) for step in range(CHIPS) for other in (0, 1) if step or other]
    for step, other in peers:
        pl.semaphore_signal(barrier, inc=1, device_id=device(step, other), device_id_type=MESH)
    for step in range(1, tp_count):
        pl.semaphore_signal(
            barrier, inc=1, device_id=(seq, (tp + step) % tp_count), device_id_type=MESH
        )

    pad = all_keys - slots - rows
    keys[pl.ds(slots + rows, pad), :] = jnp.zeros((pad, width), keys.dtype)
    values[pl.ds(slots + rows, pad), :] = jnp.zeros((pad, width), values.dtype)
    forget_tile[...] = jnp.zeros(forget_tile.shape, jnp.float32)
    logit = logit_ref[...]
    forget_tile[pl.ds(0, heads), pl.ds(0, rows)] = -jnp.log1p(jnp.exp(-logit))
    lane = lax.broadcasted_iota(jnp.int32, forget_tile.shape, 1)
    running = forget_tile[...]
    reach = 1
    while reach < rows:
        running = running + jnp.where(lane >= reach, pltpu.roll(running, reach, 1), 0.0)
        reach *= 2
    total = jnp.sum(jnp.where(lane == rows - 1, running, 0.0), axis=1, keepdims=True)
    forget_tile[...] = jnp.broadcast_to(total, forget_tile.shape)
    pl.semaphore_wait(barrier, len(peers) + tp_count - 1)

    def query_direct(step):
        return pltpu.make_async_remote_copy(
            src_ref=q_ref,
            dst_ref=queries.at[(CHIPS - step) % CHIPS, 0 if step else 1],
            send_sem=query_send.at[step, 0],
            recv_sem=query_recv.at[(CHIPS - step) % CHIPS, 0 if step else 1],
            device_id=device(step, 0 if step else 1),
            device_id_type=MESH,
        )

    def query_relay(step):
        return pltpu.make_async_remote_copy(
            src_ref=queries.at[step, 0],
            dst_ref=queries.at[step, 1],
            send_sem=query_send.at[step, 1],
            recv_sem=query_recv.at[step, 1],
            device_id=device(0, 1),
            device_id_type=MESH,
        )

    def forget_copy(step, other):
        return pltpu.make_async_remote_copy(
            src_ref=forget_tile,
            dst_ref=forget_all.at[(CHIPS - step) % CHIPS, other],
            send_sem=forget_send.at[step, other],
            recv_sem=forget_recv.at[(CHIPS - step) % CHIPS, other],
            device_id=device(step, other),
            device_id_type=MESH,
        )

    near_first = [0, 1, 7, 2, 6, 3, 5, 4]
    for step in reversed(near_first):
        query_direct(step).start()
    for step, other in peers:
        forget_copy(step, other).start()

    length = length_ref[request]
    page_lane = lax.broadcasted_iota(jnp.int32, (1, PAGE), 1)
    for page in range(slots // PAGE):
        alive = page_ref[page] * PAGE + page_lane < length
        at = pl.ds(page * PAGE, PAGE)
        costs[pl.ds(0, heads), at] = jnp.where(alive, decay_ref[:, at], DEAD)

    for step, other in peers:
        forget_copy((CHIPS - step) % CHIPS, other).wait_recv()
    own_forget = running
    for step, other in peers:
        earlier = (core == 1) if step == 0 else (chip + step >= CHIPS)
        own_forget = own_forget + jnp.where(earlier, forget_all[step, other], 0.0)
    forget_ref[...] = own_forget[:heads, :rows]
    costs[:, pl.ds(slots, PAGE)] = jnp.where(lane < rows, own_forget, DEAD)

    for step in near_first[1:]:
        query_direct((CHIPS - step) % CHIPS).wait_recv()
        query_relay(step).start()
    for copy in local:
        copy.wait()
    query_direct(0).wait_recv()

    span = 2
    chunk = span * 2 * rows
    left = lax.broadcasted_iota(jnp.int32, (chunk, 2 * HEAD_DIM), 1) < HEAD_DIM
    key_lane = lax.broadcasted_iota(jnp.int32, (chunk, PAGE), 1)
    row_index = lax.broadcasted_iota(jnp.int32, (chunk, PAGE), 0)

    def part_copy(step, other):
        return pltpu.make_async_remote_copy(
            src_ref=parts_out.at[step, other],
            dst_ref=parts_in.at[(CHIPS - step) % CHIPS, other],
            send_sem=part_send.at[step, other],
            recv_sem=part_recv.at[(CHIPS - step) % CHIPS, other],
            device_id=device(step, other),
            device_id_type=MESH,
        )

    def step_of(turn):
        return ((turn + 1) // 2 * (2 * (turn % 2) - 1) + CHIPS) % CHIPS

    def attend(index):
        steps = [step_of(index * span + i) for i in range(span)]
        fresh = None
        for i, step in enumerate(steps):
            for other in (0, 1):
                first = (2 * i + other) * rows
                offset = row_index - first
                inside = (offset >= 0) & (offset < rows)
                later = jnp.where(
                    step == 0, jnp.where(core + other == 1, 1 - core, 0), (chip + step < CHIPS) * 1
                )
                own = jnp.where(step == 0, 1 - other, 0)
                limit = jnp.where(own == 1, offset, jnp.where(later == 1, rows, -1))
                fresh = jnp.where(inside, limit, 0 if fresh is None else fresh)
        visible = key_lane <= fresh
        pieces = [
            queries[step, other] for step in steps for other in (0, 1)
        ]
        stats = []
        outs = []
        for pair in range(pairs):
            at = slice(pair * 2 * HEAD_DIM, (pair + 1) * 2 * HEAD_DIM)
            q = jnp.concatenate([piece[:, at] for piece in pieces], axis=0)
            q = q * jnp.asarray(HEAD_DIM**-0.5, q.dtype)
            zero = jnp.zeros_like(q)
            value_pair = jnp.concatenate(
                [values[:, at], jnp.ones((all_keys, 2 * HEAD_DIM), values.dtype)], axis=1
            )
            both = []
            for side in (0, 1):
                head = pair * 2 + side
                q_side = jnp.where(left, q, zero) if side == 0 else jnp.where(left, zero, q)
                scores = lax.dot_general(
                    q_side,
                    keys[:, at],
                    (((1,), (1,)), ((), ())),
                    preferred_element_type=jnp.float32,
                )
                scores = scores - costs[pl.ds(head, 1), :]
                old = scores[:, :slots]
                new = jnp.where(visible, scores[:, slots:], -DEAD)
                highest = jnp.maximum(
                    jnp.max(old, axis=1, keepdims=True), jnp.max(new, axis=1, keepdims=True)
                )
                weights = jnp.concatenate(
                    [
                        jnp.exp(old - highest).astype(jnp.bfloat16),
                        jnp.exp(new - highest).astype(jnp.bfloat16),
                    ],
                    axis=1,
                )
                summed = jnp.dot(weights, value_pair, preferred_element_type=jnp.float32)
                sums = summed[:, 2 * HEAD_DIM :]
                both.append(summed[:, : 2 * HEAD_DIM] / sums)
                stats.append(highest + jnp.log(sums))
            outs.append(jnp.where(left, both[0], both[1]).astype(jnp.bfloat16))
        stat_lane = lax.broadcasted_iota(jnp.int32, (chunk, PAGE), 1)
        packed = jnp.zeros((chunk, PAGE), jnp.float32)
        for head, stat in enumerate(stats):
            high, middle, low = (t.astype(jnp.float32) for t in thirds(stat))
            packed = jnp.where(stat_lane == head, high, packed)
            packed = jnp.where(stat_lane == head + 8, middle, packed)
            packed = jnp.where(stat_lane == head + 16, low, packed)
        outs.append(packed.astype(jnp.bfloat16))
        for i, step in enumerate(steps):
            for other in (0, 1):
                first = (2 * i + other) * rows
                for j, out in enumerate(outs):
                    parts_out[step, other, :, pl.ds(j * 2 * HEAD_DIM, 2 * HEAD_DIM)] = out[
                        first : first + rows
                    ]
        return steps

    def wait_queries(step):
        pltpu.make_async_remote_copy(
            src_ref=queries.at[step, 0],
            dst_ref=queries.at[step, 1],
            send_sem=query_send.at[step, 1],
            recv_sem=query_recv.at[step, 1],
            device_id=device(0, 1),
            device_id_type=MESH,
        ).wait_recv()

    def turn(index, _):
        for i in range(span):
            step = step_of(index * span + i)

            @pl.when(step > 0)
            def _():
                wait_queries(step)

        steps = attend(index)
        for step in steps:

            @pl.when(step > 0)
            def _():
                part_copy(step, 0).start()

            part_copy(step, 1).start()
        return 0

    lax.fori_loop(0, CHIPS // span, turn, 0)

    stat_rows = []
    for step in range(CHIPS):
        for other in (0, 1):
            if step or other:
                part_copy((CHIPS - step) % CHIPS, other).wait_recv()
    def part(step, other, at):
        source = parts_in if (step or other) else parts_out
        return source[step, other, :, at]

    logs = []
    for step in range(CHIPS):
        for other in (0, 1):
            stat = part(step, other, pl.ds(width, PAGE)).astype(jnp.float32)
            logs.append(
                stat + pltpu.roll(stat, PAGE - 8, 1) + pltpu.roll(stat, PAGE - 16, 1)
            )
    top = functools.reduce(jnp.maximum, logs)
    shares = [jnp.exp(log - top) for log in logs]
    whole = functools.reduce(jnp.add, shares)
    stacked = jnp.concatenate([share / whole for share in shares], axis=0)
    stat_lane = lax.broadcasted_iota(jnp.int32, stacked.shape, 1)
    stacked = jnp.where(stat_lane < heads, stacked, 0.0)
    high, middle, _ = thirds(stacked)
    spread_row = lax.broadcasted_iota(jnp.int32, (2 * PAGE, width), 0) % PAGE
    spread_lane = lax.broadcasted_iota(jnp.int32, (2 * PAGE, width), 1) // HEAD_DIM
    spread = jnp.where(spread_row == spread_lane, 1.0, 0.0).astype(jnp.bfloat16)
    factors = jnp.dot(
        jnp.concatenate([high, middle], axis=1), spread, preferred_element_type=jnp.float32
    )
    attention = jnp.zeros((rows, width), jnp.float32)
    for step in range(CHIPS):
        for other in (0, 1):
            first = (2 * step + other) * rows
            attention = attention + factors[first : first + rows] * part(
                step, other, pl.ds(0, width)
            ).astype(jnp.float32)
    attention = attention.astype(jnp.bfloat16)

    def share_copy(step):
        return pltpu.make_async_remote_copy(
            src_ref=shares_out.at[step - 1],
            dst_ref=shares_in.at[tp_count - step - 1],
            send_sem=share_send.at[step - 1],
            recv_sem=share_recv.at[tp_count - step - 1],
            device_id=(seq, (tp + step) % tp_count),
            device_id_type=MESH,
        )

    def share(step):
        block = (tp + step) % tp_count
        columns = pl.ds(pl.multiple_of(block * width, PAGE), width)
        return jnp.dot(attention, weight[:, columns], preferred_element_type=jnp.float32)

    for step in range(1, tp_count):
        shares_out[step - 1] = share(step).astype(jnp.bfloat16)
        share_copy(step).start()
    summed = share(0)
    for step in range(1, tp_count):
        share_copy(step).wait_recv()
        summed = summed + shares_in[tp_count - step - 1].astype(jnp.float32)
    out_ref[...] = (residual_ref[...].astype(jnp.float32) + summed).astype(out_ref.dtype)

    for step in range(CHIPS):
        query_direct(step).wait_send()
        if step:
            query_relay(step).wait_send()
    for step, other in peers:
        forget_copy(step, other).wait_send()
        part_copy(step, other).wait_send()
    for step in range(1, tp_count):
        share_copy(step).wait_send()


def shards(
    queries,
    new_keys,
    new_values,
    forget_logit,
    cache_keys,
    cache_values,
    cache_decay,
    slot_page,
    cache_len,
    residual,
    out_weight,
):
    rows, width = queries.shape
    heads = forget_logit.shape[0]
    slots = cache_keys.shape[0]
    tp_count = lax.axis_size("tp")
    vmem = pl.BlockSpec(memory_space=pltpu.VMEM)
    smem = pl.BlockSpec(memory_space=pltpu.SMEM)
    anywhere = pl.BlockSpec(memory_space=pl.ANY)
    dma = pltpu.SemaphoreType.DMA
    half = jnp.bfloat16
    single = jnp.float32
    return pl.pallas_call(
        functools.partial(layer_kernel, tp_count),
        out_shape=(
            jax.ShapeDtypeStruct((rows, width), half),
            jax.ShapeDtypeStruct((heads, rows), single),
        ),
        in_specs=[
            vmem, anywhere, anywhere, vmem, anywhere, anywhere, vmem, smem, smem, vmem, anywhere,
        ],
        out_specs=(vmem, vmem),
        scratch_shapes=[
            pltpu.VMEM((slots + PAGE, width), half),
            pltpu.VMEM((slots + PAGE, width), half),
            pltpu.VMEM(out_weight.shape, half),
            pltpu.VMEM((8, slots + PAGE), single),
            pltpu.VMEM((CHIPS, 2, rows, width), half),
            pltpu.VMEM((8, PAGE), single),
            pltpu.VMEM((CHIPS, 2, 8, PAGE), single),
            pltpu.VMEM((CHIPS, 2, rows, width + PAGE), half),
            pltpu.VMEM((CHIPS, 2, rows, width + PAGE), half),
            pltpu.VMEM((max(tp_count - 1, 1), rows, width), half),
            pltpu.VMEM((max(tp_count - 1, 1), rows, width), half),
            dma((6,)),
            dma((CHIPS, 2)),
            dma((CHIPS, 2)),
            dma((CHIPS, 2)),
            dma((CHIPS, 2)),
            dma((CHIPS, 2)),
            dma((CHIPS, 2)),
            dma((max(tp_count - 1, 1),)),
            dma((max(tp_count - 1, 1),)),
        ],
        compiler_params=pltpu.CompilerParams(
            collective_id=0, has_side_effects=True, vmem_limit_bytes=60 * 1024 * 1024
        ),
        name="layer",
    )(
        queries, new_keys, new_values, forget_logit, cache_keys, cache_values, cache_decay,
        slot_page, cache_len, residual, out_weight,
    )


def solution(mesh):
    return jax.shard_map(
        shards,
        mesh=mesh,
        in_specs=(
            P("seq", "tp"),
            P("seq", "tp"),
            P("seq", "tp"),
            P("tp", "seq"),
            P("seq", "tp"),
            P("seq", "tp"),
            P("tp", "seq"),
            P("seq"),
            P(),
            P("seq", "tp"),
            P("tp", None),
        ),
        out_specs=(P("seq", "tp"), P("tp", "seq")),
        check_vma=False,
    )
```

```python
import functools

import jax
import jax.numpy as jnp
from jax import lax
from jax.experimental import pallas as pl
from jax.experimental.pallas import tpu as pltpu
from jax.sharding import PartitionSpec as P

HEAD_DIM = 64
PAGE = 128
CHIPS = 8
GROUP = 16
DEAD = 1e30
MESH = pl.DeviceIdType.MESH


def thirds(x):
    high = x.astype(jnp.bfloat16)
    rest = x - high.astype(jnp.float32)
    middle = rest.astype(jnp.bfloat16)
    low = (rest - middle.astype(jnp.float32)).astype(jnp.bfloat16)
    return high, middle, low


def merge_weights(logs, spread, heads):
    top = functools.reduce(jnp.maximum, logs)
    shares = [jnp.exp(log - top) for log in logs]
    whole = functools.reduce(jnp.add, shares)
    stacked = jnp.concatenate([share / whole for share in shares], axis=0)
    lane = lax.broadcasted_iota(jnp.int32, stacked.shape, 1)
    stacked = jnp.where(lane < heads, stacked, 0.0)
    high, middle, _ = thirds(stacked)
    factors = jnp.dot(
        jnp.concatenate([high, middle], axis=1), spread, preferred_element_type=jnp.float32
    )
    return factors, top + jnp.log(whole)


def read_logs(stat):
    stat = stat.astype(jnp.float32)
    return stat + pltpu.roll(stat, PAGE - 8, 1) + pltpu.roll(stat, PAGE - 16, 1)


def write_logs(logs, heads):
    lane = lax.broadcasted_iota(jnp.int32, logs.shape, 1)
    high, middle, low = (
        part.astype(jnp.float32) for part in thirds(jnp.where(lane < heads, logs, 0.0))
    )
    packed = high + pltpu.roll(middle, 8, 1) + pltpu.roll(low, 16, 1)
    return packed.astype(jnp.bfloat16)


def layer_kernel(
    tp_count,
    q_ref,
    new_keys,
    new_values,
    logit_in,
    cache_keys,
    cache_values,
    decay_in,
    page_ref,
    length_ref,
    residual_in,
    out_weight,
    out_ref,
    forget_ref,
    keys,
    values,
    weight,
    logit_ref,
    decay_ref,
    residual_ref,
    costs,
    queries,
    forget_tile,
    forget_all,
    spread,
    parts_out,
    pair_in,
    merged,
    parts_in,
    shares_out,
    shares_in,
    local_sem,
    query_send,
    query_recv,
    forget_send,
    forget_recv,
    pair_send,
    pair_recv,
    part_send,
    part_recv,
    share_send,
    share_recv,
):
    rows, width = q_ref.shape
    heads = width // HEAD_DIM
    pairs = heads // 2
    slots = cache_keys.shape[0]
    all_keys = keys.shape[0]
    seq = lax.axis_index("seq")
    tp = lax.axis_index("tp")
    request = seq // GROUP
    chip = (seq % GROUP) // 2
    core = seq % 2

    def device(chip_step, other):
        there = (chip + chip_step) % CHIPS
        return (request * GROUP + there * 2 + (1 - core if other else core), tp)

    barrier = pltpu.get_barrier_semaphore()
    peers = [(step, other) for step in range(CHIPS) for other in (0, 1) if step or other]
    for step, other in peers:
        pl.semaphore_signal(barrier, inc=1, device_id=device(step, other), device_id_type=MESH)
    for step in range(1, tp_count):
        pl.semaphore_signal(
            barrier, inc=1, device_id=(seq, (tp + step) % tp_count), device_id_type=MESH
        )

    local = [
        pltpu.make_async_copy(source, target, local_sem.at[i])
        for i, (source, target) in enumerate(
            [
                (logit_in, logit_ref),
                (q_ref, queries.at[0, 0]),
                (decay_in, decay_ref),
                (new_keys, keys.at[pl.ds(slots, rows)]),
                (new_values, values.at[pl.ds(slots, rows)]),
                (cache_keys, keys.at[pl.ds(0, slots)]),
                (cache_values, values.at[pl.ds(0, slots)]),
                (out_weight, weight),
                (residual_in, residual_ref),
            ]
        )
    ]
    for copy in local:
        copy.start()

    pad = all_keys - slots - rows
    keys[pl.ds(slots + rows, pad), :] = jnp.zeros((pad, width), keys.dtype)
    values[pl.ds(slots + rows, pad), :] = jnp.zeros((pad, width), values.dtype)
    forget_tile[...] = jnp.zeros(forget_tile.shape, jnp.float32)
    spread_row = lax.broadcasted_iota(jnp.int32, spread.shape, 0) % PAGE
    spread_lane = lax.broadcasted_iota(jnp.int32, spread.shape, 1) // HEAD_DIM
    spread[...] = jnp.where(spread_row == spread_lane, 1.0, 0.0).astype(spread.dtype)
    local[0].wait()
    logit = logit_ref[...]
    forget_tile[pl.ds(0, heads), pl.ds(0, rows)] = -jnp.log1p(jnp.exp(-logit))
    lane = lax.broadcasted_iota(jnp.int32, forget_tile.shape, 1)
    running = forget_tile[...]
    reach = 1
    while reach < rows:
        running = running + jnp.where(lane >= reach, pltpu.roll(running, reach, 1), 0.0)
        reach *= 2
    total = jnp.sum(jnp.where(lane == rows - 1, running, 0.0), axis=1, keepdims=True)
    forget_tile[...] = jnp.broadcast_to(total, forget_tile.shape)
    pl.semaphore_wait(barrier, len(peers) + tp_count - 1)

    def query_direct(step, other):
        back = (CHIPS - step) % CHIPS
        return pltpu.make_async_remote_copy(
            src_ref=q_ref,
            dst_ref=queries.at[back, other],
            send_sem=query_send.at[step, other],
            recv_sem=query_recv.at[back, other],
            device_id=device(step, other),
            device_id_type=MESH,
        )

    def query_relay(step):
        return pltpu.make_async_remote_copy(
            src_ref=queries.at[step, 0],
            dst_ref=queries.at[step, 1],
            send_sem=query_send.at[8 - step, 1],
            recv_sem=query_recv.at[step, 1],
            device_id=device(0, 1),
            device_id_type=MESH,
        )

    def forget_copy(step, other):
        return pltpu.make_async_remote_copy(
            src_ref=forget_tile,
            dst_ref=forget_all.at[(CHIPS - step) % CHIPS, other],
            send_sem=forget_send.at[step, other],
            recv_sem=forget_recv.at[(CHIPS - step) % CHIPS, other],
            device_id=device(step, other),
            device_id_type=MESH,
        )

    for step, other in peers:
        forget_copy(step, other).start()
    first_sends = [(0, 1), (1, 0), (1, 1)]
    later_sends = [(step, 0) for step in (4, 5, 3, 6, 7, 2)]
    for step, other in first_sends + later_sends:
        query_direct(step, other).start()

    local[2].wait()
    length = length_ref[request]
    page_lane = lax.broadcasted_iota(jnp.int32, (1, PAGE), 1)
    for page in range(slots // PAGE):
        alive = page_ref[page] * PAGE + page_lane < length
        at = pl.ds(page * PAGE, PAGE)
        costs[pl.ds(0, heads), at] = jnp.where(alive, decay_ref[:, at], DEAD)
    for i in (1, 3, 4, 5, 6, 7, 8):
        local[i].wait()

    for step, other in peers:
        forget_copy((CHIPS - step) % CHIPS, other).wait_recv()
    own_forget = running
    for step, other in peers:
        earlier = (core == 1) if step == 0 else (chip + step >= CHIPS)
        own_forget = own_forget + jnp.where(earlier, forget_all[step, other], 0.0)
    forget_ref[...] = own_forget[:heads, :rows]
    costs[:, pl.ds(slots, PAGE)] = jnp.where(lane < rows, own_forget, DEAD)
    for step, other in first_sends:
        query_direct(step, other).wait_recv()

    span = 2
    chunk = span * 2 * rows
    left = lax.broadcasted_iota(jnp.int32, (chunk, 2 * HEAD_DIM), 1) < HEAD_DIM
    key_lane = lax.broadcasted_iota(jnp.int32, (chunk, PAGE), 1)
    row_index = lax.broadcasted_iota(jnp.int32, (chunk, PAGE), 0)

    def pair_copy(step):
        return pltpu.make_async_remote_copy(
            src_ref=parts_out.at[step, 1],
            dst_ref=pair_in.at[step],
            send_sem=pair_send.at[step],
            recv_sem=pair_recv.at[step],
            device_id=device(0, 1),
            device_id_type=MESH,
        )

    def part_copy(step):
        back = (CHIPS - step) % CHIPS
        return pltpu.make_async_remote_copy(
            src_ref=merged.at[step],
            dst_ref=parts_in.at[back],
            send_sem=part_send.at[step],
            recv_sem=part_recv.at[back],
            device_id=device(step, 0),
            device_id_type=MESH,
        )

    def steps_of(index):
        first = 2 * ((index // 2 + index % 2) % 2) + index // 2
        return [first, CHIPS - 1 - first]

    def join_pair(index):
        steps = steps_of(index)
        for step in steps:
            pair_copy(step).wait_recv()
        mine = jnp.concatenate([parts_out[step, 0] for step in steps], axis=0)
        partner = jnp.concatenate([pair_in[step] for step in steps], axis=0)
        factors, logs = merge_weights(
            [read_logs(mine[:, width:]), read_logs(partner[:, width:])], spread[...], heads
        )
        half = span * rows
        both = factors[:half] * mine[:, :width].astype(jnp.float32) + factors[
            half:
        ] * partner[:, :width].astype(jnp.float32)
        both = both.astype(jnp.bfloat16)
        stat = write_logs(logs, heads)
        for i, step in enumerate(steps):
            here = slice(i * rows, (i + 1) * rows)
            merged[step, :, pl.ds(0, width)] = both[here]
            merged[step, :, pl.ds(width, PAGE)] = stat[here]
        for step in steps:

            @pl.when(step > 0)
            def _():
                part_copy(step).start()

    def attend(index, between):
        steps = steps_of(index)
        fresh = None
        for i, step in enumerate(steps):
            for other in (0, 1):
                first = (2 * i + other) * rows
                offset = row_index - first
                inside = (offset >= 0) & (offset < rows)
                later = jnp.where(
                    step == 0, jnp.where(core + other == 1, 1 - core, 0), (chip + step < CHIPS) * 1
                )
                own = jnp.where(step == 0, 1 - other, 0)
                limit = jnp.where(own == 1, offset, jnp.where(later == 1, rows, -1))
                fresh = jnp.where(inside, limit, 0 if fresh is None else fresh)
        visible = key_lane <= fresh
        packed = jnp.zeros((chunk, PAGE), jnp.float32)
        for pair in range(pairs):
            if pair == pairs - 1:
                between()
            at = slice(pair * 2 * HEAD_DIM, (pair + 1) * 2 * HEAD_DIM)
            q = jnp.concatenate(
                [queries[step, other, :, at] for step in steps for other in (0, 1)], axis=0
            )
            q = q * jnp.asarray(HEAD_DIM**-0.5, q.dtype)
            zero = jnp.zeros_like(q)
            value_pair = jnp.concatenate(
                [values[:, at], jnp.ones((all_keys, 2 * HEAD_DIM), values.dtype)], axis=1
            )
            both = []
            for side in (0, 1):
                head = pair * 2 + side
                q_side = jnp.where(left, q, zero) if side == 0 else jnp.where(left, zero, q)
                scores = lax.dot_general(
                    q_side,
                    keys[:, at],
                    (((1,), (1,)), ((), ())),
                    preferred_element_type=jnp.float32,
                )
                scores = scores - costs[pl.ds(head, 1), :]
                old = scores[:, :slots]
                new = jnp.where(visible, scores[:, slots:], -DEAD)
                highest = jnp.maximum(
                    jnp.max(old, axis=1, keepdims=True), jnp.max(new, axis=1, keepdims=True)
                )
                weights = jnp.concatenate(
                    [
                        jnp.exp(old - highest).astype(jnp.bfloat16),
                        jnp.exp(new - highest).astype(jnp.bfloat16),
                    ],
                    axis=1,
                )
                summed = jnp.dot(weights, value_pair, preferred_element_type=jnp.float32)
                sums = summed[:, 2 * HEAD_DIM :]
                both.append(summed[:, : 2 * HEAD_DIM] / sums)
                packed = jnp.where(key_lane == head, highest + jnp.log(sums), packed)
            out = jnp.where(left, both[0], both[1]).astype(jnp.bfloat16)
            for i in range(2 * span):
                parts_out[steps[i // 2], i % 2, :, at] = out[i * rows : (i + 1) * rows]
        stat = write_logs(packed, heads)
        for i in range(2 * span):
            parts_out[steps[i // 2], i % 2, :, pl.ds(width, PAGE)] = stat[
                i * rows : (i + 1) * rows
            ]
        for step in steps:
            pair_copy(step).start()

    turns = CHIPS // span

    def turn(index, _):
        @pl.when(index > 0)
        def _():
            for step in steps_of(index):
                query_relay(step).wait_recv()

        def between():
            @pl.when(index < turns - 1)
            def _():
                for step in steps_of(index + 1):
                    query_direct(CHIPS - step, 0).wait_recv()
                    query_relay(step).start()

            @pl.when(index > 0)
            def _():
                join_pair(index - 1)

        attend(index, between)
        return 0

    lax.fori_loop(0, turns, turn, 0)
    join_pair(turns - 1)

    for step in range(1, CHIPS):
        part_copy(CHIPS - step).wait_recv()

    def part(step, at):
        return parts_in[step, :, at] if step else merged[0, :, at]

    factors, _ = merge_weights(
        [read_logs(part(step, pl.ds(width, PAGE))) for step in range(CHIPS)], spread[...], heads
    )
    attention = jnp.zeros((rows, width), jnp.float32)
    for step in range(CHIPS):
        attention = attention + factors[step * rows : (step + 1) * rows] * part(
            step, pl.ds(0, width)
        ).astype(jnp.float32)
    attention = attention.astype(jnp.bfloat16)

    def share_copy(step):
        return pltpu.make_async_remote_copy(
            src_ref=shares_out.at[step - 1],
            dst_ref=shares_in.at[tp_count - step - 1],
            send_sem=share_send.at[step - 1],
            recv_sem=share_recv.at[tp_count - step - 1],
            device_id=(seq, (tp + step) % tp_count),
            device_id_type=MESH,
        )

    def share(step):
        block = (tp + step) % tp_count
        columns = pl.ds(pl.multiple_of(block * width, PAGE), width)
        return jnp.dot(attention, weight[:, columns], preferred_element_type=jnp.float32)

    for step in (2, 1, 3)[: tp_count - 1]:
        shares_out[step - 1] = share(step).astype(jnp.bfloat16)
        share_copy(step).start()
    summed = share(0) + residual_ref[...].astype(jnp.float32)
    for step in range(1, tp_count):
        share_copy(step).wait_recv()
        summed = summed + shares_in[tp_count - step - 1].astype(jnp.float32)
    out_ref[...] = summed.astype(out_ref.dtype)

    for step, other in first_sends + later_sends:
        query_direct(step, other).wait_send()
    for step in range(1, CHIPS - 1):
        query_relay(step).wait_send()
    for step, other in peers:
        forget_copy(step, other).wait_send()
    for step in range(CHIPS):
        pair_copy(step).wait_send()
        if step:
            part_copy(step).wait_send()
    for step in range(1, tp_count):
        share_copy(step).wait_send()


def shards(
    queries,
    new_keys,
    new_values,
    forget_logit,
    cache_keys,
    cache_values,
    cache_decay,
    slot_page,
    cache_len,
    residual,
    out_weight,
):
    rows, width = queries.shape
    heads = forget_logit.shape[0]
    slots = cache_keys.shape[0]
    tp_count = lax.axis_size("tp")
    vmem = pl.BlockSpec(memory_space=pltpu.VMEM)
    smem = pl.BlockSpec(memory_space=pltpu.SMEM)
    anywhere = pl.BlockSpec(memory_space=pl.ANY)
    dma = pltpu.SemaphoreType.DMA
    half = jnp.bfloat16
    single = jnp.float32
    return pl.pallas_call(
        functools.partial(layer_kernel, tp_count),
        out_shape=(
            jax.ShapeDtypeStruct((rows, width), half),
            jax.ShapeDtypeStruct((heads, rows), single),
        ),
        in_specs=[
            anywhere, anywhere, anywhere, anywhere, anywhere, anywhere, anywhere, smem, smem,
            anywhere, anywhere,
        ],
        out_specs=(vmem, vmem),
        scratch_shapes=[
            pltpu.VMEM((slots + PAGE, width), half),
            pltpu.VMEM((slots + PAGE, width), half),
            pltpu.VMEM(out_weight.shape, half),
            pltpu.VMEM(forget_logit.shape, single),
            pltpu.VMEM(cache_decay.shape, single),
            pltpu.VMEM(residual.shape, half),
            pltpu.VMEM((8, slots + PAGE), single),
            pltpu.VMEM((CHIPS, 2, rows, width), half),
            pltpu.VMEM((8, PAGE), single),
            pltpu.VMEM((CHIPS, 2, 8, PAGE), single),
            pltpu.VMEM((2 * PAGE, width), half),
            pltpu.VMEM((CHIPS, 2, rows, width + PAGE), half),
            pltpu.VMEM((CHIPS, rows, width + PAGE), half),
            pltpu.VMEM((CHIPS, rows, width + PAGE), half),
            pltpu.VMEM((CHIPS, rows, width + PAGE), half),
            pltpu.VMEM((max(tp_count - 1, 1), rows, width), half),
            pltpu.VMEM((max(tp_count - 1, 1), rows, width), half),
            dma((9,)),
            dma((CHIPS, 2)),
            dma((CHIPS, 2)),
            dma((CHIPS, 2)),
            dma((CHIPS, 2)),
            dma((CHIPS,)),
            dma((CHIPS,)),
            dma((CHIPS,)),
            dma((CHIPS,)),
            dma((max(tp_count - 1, 1),)),
            dma((max(tp_count - 1, 1),)),
        ],
        compiler_params=pltpu.CompilerParams(
            collective_id=0, has_side_effects=True, vmem_limit_bytes=60 * 1024 * 1024
        ),
        name="layer",
    )(
        queries, new_keys, new_values, forget_logit, cache_keys, cache_values, cache_decay,
        slot_page, cache_len, residual, out_weight,
    )


def solution(mesh):
    return jax.shard_map(
        shards,
        mesh=mesh,
        in_specs=(
            P("seq", "tp"),
            P("seq", "tp"),
            P("seq", "tp"),
            P("tp", "seq"),
            P("seq", "tp"),
            P("seq", "tp"),
            P("tp", "seq"),
            P("seq"),
            P(),
            P("seq", "tp"),
            P("tp", None),
        ),
        out_specs=(P("seq", "tp"), P("tp", "seq")),
        check_vma=False,
    )
```

```python
import functools

import jax
import jax.numpy as jnp
from jax import lax
from jax.experimental import pallas as pl
from jax.experimental.pallas import tpu as pltpu
from jax.sharding import PartitionSpec as P

HEAD_DIM = 64
PAGE = 128
CHIPS = 8
GROUP = 16
DEAD = 1e30
BETWEEN = 4
MESH = pl.DeviceIdType.MESH


def thirds(x):
    high = x.astype(jnp.bfloat16)
    rest = x - high.astype(jnp.float32)
    middle = rest.astype(jnp.bfloat16)
    low = (rest - middle.astype(jnp.float32)).astype(jnp.bfloat16)
    return high, middle, low


def merge_weights(logs, spread, heads):
    top = functools.reduce(jnp.maximum, logs)
    shares = [jnp.exp(log - top) for log in logs]
    whole = functools.reduce(jnp.add, shares)
    stacked = jnp.concatenate([share / whole for share in shares], axis=0)
    lane = lax.broadcasted_iota(jnp.int32, stacked.shape, 1)
    stacked = jnp.where(lane < heads, stacked, 0.0)
    high, middle, _ = thirds(stacked)
    factors = jnp.dot(
        jnp.concatenate([high, middle], axis=1), spread, preferred_element_type=jnp.float32
    )
    return factors, top + jnp.log(whole)


def read_logs(stat):
    stat = stat.astype(jnp.float32)
    return stat + pltpu.roll(stat, PAGE - 8, 1) + pltpu.roll(stat, PAGE - 16, 1)


def write_logs(logs, heads):
    lane = lax.broadcasted_iota(jnp.int32, logs.shape, 1)
    high, middle, low = (
        part.astype(jnp.float32) for part in thirds(jnp.where(lane < heads, logs, 0.0))
    )
    packed = high + pltpu.roll(middle, 8, 1) + pltpu.roll(low, 16, 1)
    return packed.astype(jnp.bfloat16)


def layer_kernel(
    tp_count,
    q_ref,
    new_keys,
    new_values,
    logit_in,
    cache_keys,
    cache_values,
    decay_in,
    page_ref,
    length_ref,
    residual_in,
    out_weight,
    out_ref,
    forget_ref,
    keys,
    values,
    weight,
    logit_ref,
    decay_ref,
    residual_ref,
    costs,
    queries,
    forget_tile,
    forget_row,
    forget_all,
    spread,
    parts_out,
    pair_in,
    merged,
    parts_in,
    shares_out,
    shares_in,
    local_sem,
    query_send,
    query_recv,
    forget_send,
    forget_recv,
    pair_send,
    pair_recv,
    part_send,
    part_recv,
    share_send,
    share_recv,
):
    rows, width = q_ref.shape
    heads = width // HEAD_DIM
    pairs = heads // 2
    slots = cache_keys.shape[0]
    all_keys = keys.shape[0]
    seq = lax.axis_index("seq")
    tp = lax.axis_index("tp")
    request = seq // GROUP
    chip = (seq % GROUP) // 2
    core = seq % 2

    def device(chip_step, other):
        there = (chip + chip_step) % CHIPS
        return (request * GROUP + there * 2 + (1 - core if other else core), tp)

    barrier = pltpu.get_barrier_semaphore()
    peers = [(step, other) for step in range(CHIPS) for other in (0, 1) if step or other]
    for step, other in peers:
        pl.semaphore_signal(barrier, inc=1, device_id=device(step, other), device_id_type=MESH)
    for step in range(1, tp_count):
        pl.semaphore_signal(
            barrier, inc=1, device_id=(seq, (tp + step) % tp_count), device_id_type=MESH
        )

    local = [
        pltpu.make_async_copy(source, target, local_sem.at[i])
        for i, (source, target) in enumerate(
            [
                (logit_in, logit_ref),
                (q_ref, queries.at[0, 0]),
                (decay_in, decay_ref),
                (new_keys, keys.at[pl.ds(slots, rows)]),
                (new_values, values.at[pl.ds(slots, rows)]),
                (cache_keys, keys.at[pl.ds(0, slots)]),
                (cache_values, values.at[pl.ds(0, slots)]),
                (out_weight, weight),
                (residual_in, residual_ref),
            ]
        )
    ]
    for copy in local:
        copy.start()

    pad = all_keys - slots - rows
    keys[pl.ds(slots + rows, pad), :] = jnp.zeros((pad, width), keys.dtype)
    values[pl.ds(slots + rows, pad), :] = jnp.zeros((pad, width), values.dtype)
    forget_tile[...] = jnp.zeros(forget_tile.shape, jnp.float32)
    spread_row = lax.broadcasted_iota(jnp.int32, spread.shape, 0) % PAGE
    spread_lane = lax.broadcasted_iota(jnp.int32, spread.shape, 1) // HEAD_DIM
    spread[...] = jnp.where(spread_row == spread_lane, 1.0, 0.0).astype(spread.dtype)
    local[0].wait()
    logit = logit_ref[...]
    forget_tile[pl.ds(0, heads), pl.ds(0, rows)] = -jnp.log1p(jnp.exp(-logit))
    lane = lax.broadcasted_iota(jnp.int32, forget_tile.shape, 1)
    running = forget_tile[...]
    reach = 1
    while reach < rows:
        running = running + jnp.where(lane >= reach, pltpu.roll(running, reach, 1), 0.0)
        reach *= 2
    total = jnp.sum(jnp.where(lane == rows - 1, running, 0.0), axis=1, keepdims=True)
    head_row = lax.broadcasted_iota(jnp.int32, forget_tile.shape, 0)
    forget_row[...] = jnp.sum(jnp.where(head_row == lane, total, 0.0), axis=0, keepdims=True)
    pl.semaphore_wait(barrier, len(peers) + tp_count - 1)

    def query_direct(step, other):
        back = (CHIPS - step) % CHIPS
        return pltpu.make_async_remote_copy(
            src_ref=q_ref,
            dst_ref=queries.at[back, other],
            send_sem=query_send.at[step, other],
            recv_sem=query_recv.at[back, other],
            device_id=device(step, other),
            device_id_type=MESH,
        )

    def query_relay(step):
        return pltpu.make_async_remote_copy(
            src_ref=queries.at[step, 0],
            dst_ref=queries.at[step, 1],
            send_sem=query_send.at[8 - step, 1],
            recv_sem=query_recv.at[step, 1],
            device_id=device(0, 1),
            device_id_type=MESH,
        )

    def forget_copy(step, other):
        return pltpu.make_async_remote_copy(
            src_ref=forget_row,
            dst_ref=forget_all.at[(CHIPS - step) % CHIPS, other],
            send_sem=forget_send.at[step, other],
            recv_sem=forget_recv.at[(CHIPS - step) % CHIPS, other],
            device_id=device(step, other),
            device_id_type=MESH,
        )

    for step, other in peers:
        forget_copy(step, other).start()
    first_sends = [(0, 1), (6, 0), (6, 1)]
    later_sends = [(step, 0) for step in (4, 3, 5, 2, 7, 1)]
    for step, other in first_sends + later_sends:
        query_direct(step, other).start()

    local[2].wait()
    length = length_ref[request]
    page_lane = lax.broadcasted_iota(jnp.int32, (1, PAGE), 1)
    for page in range(slots // PAGE):
        alive = page_ref[page] * PAGE + page_lane < length
        at = pl.ds(page * PAGE, PAGE)
        costs[pl.ds(0, heads), at] = jnp.where(alive, decay_ref[:, at], DEAD)
    for i in (1, 3, 4, 5, 6, 7, 8):
        local[i].wait()

    for step, other in peers:
        forget_copy((CHIPS - step) % CHIPS, other).wait_recv()
    before = jnp.zeros(forget_row.shape, jnp.float32)
    for step, other in peers:
        earlier = (core == 1) if step == 0 else (chip + step >= CHIPS)
        before = before + jnp.where(earlier, forget_all[step, other], 0.0)
    own_forget = running + jnp.sum(
        jnp.where(head_row == lane, before, 0.0), axis=1, keepdims=True
    )
    forget_ref[...] = own_forget[:heads, :rows]
    costs[:, pl.ds(slots, PAGE)] = jnp.where(lane < rows, own_forget, DEAD)
    for step, other in first_sends:
        query_direct(step, other).wait_recv()

    span = 2
    chunk = span * 2 * rows
    left = lax.broadcasted_iota(jnp.int32, (chunk, 2 * HEAD_DIM), 1) < HEAD_DIM
    key_lane = lax.broadcasted_iota(jnp.int32, (chunk, PAGE), 1)
    row_index = lax.broadcasted_iota(jnp.int32, (chunk, PAGE), 0)

    def pair_copy(step):
        return pltpu.make_async_remote_copy(
            src_ref=parts_out.at[step, 1],
            dst_ref=pair_in.at[step],
            send_sem=pair_send.at[step],
            recv_sem=pair_recv.at[step],
            device_id=device(0, 1),
            device_id_type=MESH,
        )

    def part_copy(step):
        back = (CHIPS - step) % CHIPS
        return pltpu.make_async_remote_copy(
            src_ref=merged.at[step],
            dst_ref=parts_in.at[back],
            send_sem=part_send.at[step],
            recv_sem=part_recv.at[back],
            device_id=device(step, 0),
            device_id_type=MESH,
        )

    def steps_of(index):
        later = (index + 3) // 4
        return [later * (4 - index * (index - 1) // 2), 2 + later * (2 + index)]

    def join_pair(index):
        steps = steps_of(index)
        for step in steps:
            pair_copy(step).wait_recv()
        mine = jnp.concatenate([parts_out[step, 0] for step in steps], axis=0)
        partner = jnp.concatenate([pair_in[step] for step in steps], axis=0)
        factors, logs = merge_weights(
            [read_logs(mine[:, width:]), read_logs(partner[:, width:])], spread[...], heads
        )
        half = span * rows
        both = factors[:half] * mine[:, :width].astype(jnp.float32) + factors[
            half:
        ] * partner[:, :width].astype(jnp.float32)
        both = both.astype(jnp.bfloat16)
        stat = write_logs(logs, heads)
        for i, step in enumerate(steps):
            here = slice(i * rows, (i + 1) * rows)
            merged[step, :, pl.ds(0, width)] = both[here]
            merged[step, :, pl.ds(width, PAGE)] = stat[here]
        for step in steps:

            @pl.when(step > 0)
            def _():
                part_copy(step).start()

    def attend(index, between):
        steps = steps_of(index)
        fresh = None
        for i, step in enumerate(steps):
            for other in (0, 1):
                first = (2 * i + other) * rows
                offset = row_index - first
                inside = (offset >= 0) & (offset < rows)
                later = jnp.where(
                    step == 0, jnp.where(core + other == 1, 1 - core, 0), (chip + step < CHIPS) * 1
                )
                own = jnp.where(step == 0, 1 - other, 0)
                limit = jnp.where(own == 1, offset, jnp.where(later == 1, rows, -1))
                fresh = jnp.where(inside, limit, 0 if fresh is None else fresh)
        visible = key_lane <= fresh
        packed = jnp.zeros((chunk, PAGE), jnp.float32)

        def columns(pair):
            return slice(pair * 2 * HEAD_DIM, (pair + 1) * 2 * HEAD_DIM)

        def scores_of(head):
            at = columns(head // 2)
            q = jnp.concatenate(
                [queries[step, other, :, at] for step in steps for other in (0, 1)], axis=0
            )
            q = q * jnp.asarray(HEAD_DIM**-0.5, q.dtype)
            zero = jnp.zeros_like(q)
            q = jnp.where(left, zero, q) if head % 2 else jnp.where(left, q, zero)
            return lax.dot_general(
                q, keys[:, at], (((1,), (1,)), ((), ())), preferred_element_type=jnp.float32
            )

        def weigh(head, scores):
            cost = costs[pl.ds(head, 1), :]
            old = scores[:, :slots] - cost[:, :slots]
            new = jnp.where(visible, scores[:, slots:] - cost[:, slots:], -DEAD)
            highest = jnp.maximum(
                jnp.max(old, axis=1, keepdims=True), jnp.max(new, axis=1, keepdims=True)
            )
            weights = jnp.concatenate(
                [
                    jnp.exp(old - highest).astype(jnp.bfloat16),
                    jnp.exp(new - highest).astype(jnp.bfloat16),
                ],
                axis=1,
            )
            value_pair = jnp.concatenate(
                [
                    values[:, columns(head // 2)],
                    jnp.ones((all_keys, 2 * HEAD_DIM), values.dtype),
                ],
                axis=1,
            )
            summed = jnp.dot(weights, value_pair, preferred_element_type=jnp.float32)
            sums = summed[:, 2 * HEAD_DIM :]
            return summed[:, : 2 * HEAD_DIM] / sums, highest + jnp.log(sums)

        ahead = scores_of(0)
        for pair in range(pairs):
            at = columns(pair)
            both = []
            for head in (2 * pair, 2 * pair + 1):
                if head == BETWEEN:
                    between()
                scores = ahead
                ahead = scores_of(head + 1) if head + 1 < heads else None
                mean, log = weigh(head, scores)
                both.append(mean)
                packed = jnp.where(key_lane == head, log, packed)
            out = jnp.where(left, both[0], both[1]).astype(jnp.bfloat16)
            for i in range(2 * span):
                parts_out[steps[i // 2], i % 2, :, at] = out[i * rows : (i + 1) * rows]
        stat = write_logs(packed, heads)
        for i in range(2 * span):
            parts_out[steps[i // 2], i % 2, :, pl.ds(width, PAGE)] = stat[
                i * rows : (i + 1) * rows
            ]
        for step in steps:
            pair_copy(step).start()

    turns = CHIPS // span

    def turn(index, _):
        @pl.when(index > 0)
        def _():
            for step in steps_of(index):
                query_relay(step).wait_recv()

        def between():
            @pl.when(index < turns - 1)
            def _():
                for step in steps_of(index + 1):
                    query_direct(CHIPS - step, 0).wait_recv()
                    query_relay(step).start()

            @pl.when(index > 0)
            def _():
                join_pair(index - 1)

        attend(index, between)
        return 0

    lax.fori_loop(0, turns, turn, 0)
    join_pair(turns - 1)

    for step in range(1, CHIPS):
        part_copy(CHIPS - step).wait_recv()

    def part(step, at):
        return parts_in[step, :, at] if step else merged[0, :, at]

    factors, _ = merge_weights(
        [read_logs(part(step, pl.ds(width, PAGE))) for step in range(CHIPS)], spread[...], heads
    )
    attention = jnp.zeros((rows, width), jnp.float32)
    for step in range(CHIPS):
        attention = attention + factors[step * rows : (step + 1) * rows] * part(
            step, pl.ds(0, width)
        ).astype(jnp.float32)
    attention = attention.astype(jnp.bfloat16)

    def share_copy(step):
        return pltpu.make_async_remote_copy(
            src_ref=shares_out.at[step - 1],
            dst_ref=shares_in.at[tp_count - step - 1],
            send_sem=share_send.at[step - 1],
            recv_sem=share_recv.at[tp_count - step - 1],
            device_id=(seq, (tp + step) % tp_count),
            device_id_type=MESH,
        )

    def share(step):
        block = (tp + step) % tp_count
        columns = pl.ds(pl.multiple_of(block * width, PAGE), width)
        return jnp.dot(attention, weight[:, columns], preferred_element_type=jnp.float32)

    for step in (2, 1, 3)[: tp_count - 1]:
        shares_out[step - 1] = share(step).astype(jnp.bfloat16)
        share_copy(step).start()
    summed = share(0) + residual_ref[...].astype(jnp.float32)
    for step in range(1, tp_count):
        share_copy(step).wait_recv()
        summed = summed + shares_in[tp_count - step - 1].astype(jnp.float32)
    out_ref[...] = summed.astype(out_ref.dtype)

    for step, other in first_sends + later_sends:
        query_direct(step, other).wait_send()
    for step in (1, 3, 4, 5, 6, 7):
        query_relay(step).wait_send()
    for step, other in peers:
        forget_copy(step, other).wait_send()
    for step in range(CHIPS):
        pair_copy(step).wait_send()
        if step:
            part_copy(step).wait_send()
    for step in range(1, tp_count):
        share_copy(step).wait_send()


def shards(
    queries,
    new_keys,
    new_values,
    forget_logit,
    cache_keys,
    cache_values,
    cache_decay,
    slot_page,
    cache_len,
    residual,
    out_weight,
):
    rows, width = queries.shape
    heads = forget_logit.shape[0]
    slots = cache_keys.shape[0]
    tp_count = lax.axis_size("tp")
    vmem = pl.BlockSpec(memory_space=pltpu.VMEM)
    smem = pl.BlockSpec(memory_space=pltpu.SMEM)
    anywhere = pl.BlockSpec(memory_space=pl.ANY)
    dma = pltpu.SemaphoreType.DMA
    half = jnp.bfloat16
    single = jnp.float32
    return pl.pallas_call(
        functools.partial(layer_kernel, tp_count),
        out_shape=(
            jax.ShapeDtypeStruct((rows, width), half),
            jax.ShapeDtypeStruct((heads, rows), single),
        ),
        in_specs=[
            anywhere, anywhere, anywhere, anywhere, anywhere, anywhere, anywhere, smem, smem,
            anywhere, anywhere,
        ],
        out_specs=(vmem, vmem),
        scratch_shapes=[
            pltpu.VMEM((slots + PAGE, width), half),
            pltpu.VMEM((slots + PAGE, width), half),
            pltpu.VMEM(out_weight.shape, half),
            pltpu.VMEM(forget_logit.shape, single),
            pltpu.VMEM(cache_decay.shape, single),
            pltpu.VMEM(residual.shape, half),
            pltpu.VMEM((8, slots + PAGE), single),
            pltpu.VMEM((CHIPS, 2, rows, width), half),
            pltpu.VMEM((8, PAGE), single),
            pltpu.VMEM((1, PAGE), single),
            pltpu.VMEM((CHIPS, 2, 1, PAGE), single),
            pltpu.VMEM((2 * PAGE, width), half),
            pltpu.VMEM((CHIPS, 2, rows, width + PAGE), half),
            pltpu.VMEM((CHIPS, rows, width + PAGE), half),
            pltpu.VMEM((CHIPS, rows, width + PAGE), half),
            pltpu.VMEM((CHIPS, rows, width + PAGE), half),
            pltpu.VMEM((max(tp_count - 1, 1), rows, width), half),
            pltpu.VMEM((max(tp_count - 1, 1), rows, width), half),
            dma((9,)),
            dma((CHIPS, 2)),
            dma((CHIPS, 2)),
            dma((CHIPS, 2)),
            dma((CHIPS, 2)),
            dma((CHIPS,)),
            dma((CHIPS,)),
            dma((CHIPS,)),
            dma((CHIPS,)),
            dma((max(tp_count - 1, 1),)),
            dma((max(tp_count - 1, 1),)),
        ],
        compiler_params=pltpu.CompilerParams(
            collective_id=0, has_side_effects=True, vmem_limit_bytes=60 * 1024 * 1024
        ),
        name="layer",
    )(
        queries, new_keys, new_values, forget_logit, cache_keys, cache_values, cache_decay,
        slot_page, cache_len, residual, out_weight,
    )


def solution(mesh):
    return jax.shard_map(
        shards,
        mesh=mesh,
        in_specs=(
            P("seq", "tp"),
            P("seq", "tp"),
            P("seq", "tp"),
            P("tp", "seq"),
            P("seq", "tp"),
            P("seq", "tp"),
            P("tp", "seq"),
            P("seq"),
            P(),
            P("seq", "tp"),
            P("tp", None),
        ),
        out_specs=(P("seq", "tp"), P("tp", "seq")),
        check_vma=False,
    )
```

```python
import functools

import jax
import jax.numpy as jnp
from jax import lax
from jax.experimental import pallas as pl
from jax.experimental.pallas import tpu as pltpu
from jax.sharding import PartitionSpec as P

HEAD_DIM = 64
PAGE = 128
CHIPS = 8
GROUP = 16
DEAD = 1e30
BETWEEN = 3
MESH = pl.DeviceIdType.MESH


def thirds(x):
    high = x.astype(jnp.bfloat16)
    rest = x - high.astype(jnp.float32)
    middle = rest.astype(jnp.bfloat16)
    low = (rest - middle.astype(jnp.float32)).astype(jnp.bfloat16)
    return high, middle, low


def merge_weights(logs, spread, heads):
    top = functools.reduce(jnp.maximum, logs)
    shares = [jnp.exp(log - top) for log in logs]
    whole = functools.reduce(jnp.add, shares)
    stacked = jnp.concatenate([share / whole for share in shares], axis=0)
    lane = lax.broadcasted_iota(jnp.int32, stacked.shape, 1)
    stacked = jnp.where(lane < heads, stacked, 0.0)
    high, middle, _ = thirds(stacked)
    factors = jnp.dot(
        jnp.concatenate([high, middle], axis=1), spread, preferred_element_type=jnp.float32
    )
    return factors, top + jnp.log(whole)


def read_logs(stat):
    stat = stat.astype(jnp.float32)
    return stat + pltpu.roll(stat, PAGE - 8, 1) + pltpu.roll(stat, PAGE - 16, 1)


def write_logs(logs, heads):
    lane = lax.broadcasted_iota(jnp.int32, logs.shape, 1)
    high, middle, low = (
        part.astype(jnp.float32) for part in thirds(jnp.where(lane < heads, logs, 0.0))
    )
    packed = high + pltpu.roll(middle, 8, 1) + pltpu.roll(low, 16, 1)
    return packed.astype(jnp.bfloat16)


def layer_kernel(
    tp_count,
    q_ref,
    new_keys,
    new_values,
    logit_in,
    cache_keys,
    cache_values,
    decay_in,
    page_ref,
    length_ref,
    residual_in,
    out_weight,
    out_ref,
    forget_ref,
    keys,
    values,
    weight,
    logit_ref,
    decay_ref,
    residual_ref,
    costs,
    queries,
    forget_tile,
    forget_row,
    forget_all,
    spread,
    parts_out,
    pair_in,
    merged,
    parts_in,
    last_in,
    shares_out,
    shares_in,
    local_sem,
    query_send,
    query_recv,
    forget_send,
    forget_recv,
    pair_send,
    pair_recv,
    part_send,
    part_recv,
    last_send,
    last_recv,
    share_send,
    share_recv,
):
    rows, width = q_ref.shape
    heads = width // HEAD_DIM
    pairs = heads // 2
    slots = cache_keys.shape[0]
    all_keys = keys.shape[0]
    seq = lax.axis_index("seq")
    tp = lax.axis_index("tp")
    request = seq // GROUP
    chip = (seq % GROUP) // 2
    core = seq % 2

    def device(chip_step, other):
        there = (chip + chip_step) % CHIPS
        return (request * GROUP + there * 2 + (1 - core if other else core), tp)

    barrier = pltpu.get_barrier_semaphore()
    peers = [(step, other) for step in range(CHIPS) for other in (0, 1) if step or other]
    for step, other in peers:
        pl.semaphore_signal(barrier, inc=1, device_id=device(step, other), device_id_type=MESH)
    for step in range(1, tp_count):
        pl.semaphore_signal(
            barrier, inc=1, device_id=(seq, (tp + step) % tp_count), device_id_type=MESH
        )

    local = [
        pltpu.make_async_copy(source, target, local_sem.at[i])
        for i, (source, target) in enumerate(
            [
                (logit_in, logit_ref),
                (q_ref, queries.at[0, 0]),
                (decay_in, decay_ref),
                (new_keys, keys.at[pl.ds(slots, rows)]),
                (new_values, values.at[pl.ds(slots, rows)]),
                (cache_keys, keys.at[pl.ds(0, slots)]),
                (cache_values, values.at[pl.ds(0, slots)]),
                (out_weight, weight),
                (residual_in, residual_ref),
            ]
        )
    ]
    for copy in local:
        copy.start()

    pad = all_keys - slots - rows
    keys[pl.ds(slots + rows, pad), :] = jnp.zeros((pad, width), keys.dtype)
    values[pl.ds(slots + rows, pad), :] = jnp.zeros((pad, width), values.dtype)
    forget_tile[...] = jnp.zeros(forget_tile.shape, jnp.float32)
    spread_row = lax.broadcasted_iota(jnp.int32, spread.shape, 0) % PAGE
    spread_lane = lax.broadcasted_iota(jnp.int32, spread.shape, 1) // HEAD_DIM
    spread[...] = jnp.where(spread_row == spread_lane, 1.0, 0.0).astype(spread.dtype)
    local[0].wait()
    logit = logit_ref[...]
    forget_tile[pl.ds(0, heads), pl.ds(0, rows)] = -jnp.log1p(jnp.exp(-logit))
    lane = lax.broadcasted_iota(jnp.int32, forget_tile.shape, 1)
    running = forget_tile[...]
    reach = 1
    while reach < rows:
        running = running + jnp.where(lane >= reach, pltpu.roll(running, reach, 1), 0.0)
        reach *= 2
    total = jnp.sum(jnp.where(lane == rows - 1, running, 0.0), axis=1, keepdims=True)
    head_row = lax.broadcasted_iota(jnp.int32, forget_tile.shape, 0)
    forget_row[...] = jnp.sum(jnp.where(head_row == lane, total, 0.0), axis=0, keepdims=True)
    pl.semaphore_wait(barrier, len(peers) + tp_count - 1)

    def query_direct(step, other):
        back = (CHIPS - step) % CHIPS
        return pltpu.make_async_remote_copy(
            src_ref=q_ref,
            dst_ref=queries.at[back, other],
            send_sem=query_send.at[step, other],
            recv_sem=query_recv.at[back, other],
            device_id=device(step, other),
            device_id_type=MESH,
        )

    def query_relay(step):
        return pltpu.make_async_remote_copy(
            src_ref=queries.at[step, 0],
            dst_ref=queries.at[step, 1],
            send_sem=query_send.at[8 - step, 1],
            recv_sem=query_recv.at[step, 1],
            device_id=device(0, 1),
            device_id_type=MESH,
        )

    def forget_copy(step, other):
        return pltpu.make_async_remote_copy(
            src_ref=forget_row,
            dst_ref=forget_all.at[(CHIPS - step) % CHIPS, other],
            send_sem=forget_send.at[step, other],
            recv_sem=forget_recv.at[(CHIPS - step) % CHIPS, other],
            device_id=device(step, other),
            device_id_type=MESH,
        )

    for step, other in peers:
        forget_copy(step, other).start()
    first_sends = [(0, 1), (6, 0), (6, 1)]
    later_sends = [(step, 0) for step in (4, 3, 5, 2, 7, 1)]
    for step, other in first_sends + later_sends:
        query_direct(step, other).start()

    local[2].wait()
    length = length_ref[request]
    page_lane = lax.broadcasted_iota(jnp.int32, (1, PAGE), 1)
    for page in range(slots // PAGE):
        alive = page_ref[page] * PAGE + page_lane < length
        at = pl.ds(page * PAGE, PAGE)
        costs[pl.ds(0, heads), at] = jnp.where(alive, decay_ref[:, at], DEAD)
    for i in (1, 3, 4, 5, 6, 7, 8):
        local[i].wait()

    for step, other in peers:
        forget_copy((CHIPS - step) % CHIPS, other).wait_recv()
    before = jnp.zeros(forget_row.shape, jnp.float32)
    for step, other in peers:
        earlier = (core == 1) if step == 0 else (chip + step >= CHIPS)
        before = before + jnp.where(earlier, forget_all[step, other], 0.0)
    own_forget = running + jnp.sum(
        jnp.where(head_row == lane, before, 0.0), axis=1, keepdims=True
    )
    forget_ref[...] = own_forget[:heads, :rows]
    costs[:, pl.ds(slots, PAGE)] = jnp.where(lane < rows, own_forget, DEAD)
    for step, other in first_sends:
        query_direct(step, other).wait_recv()

    span = 2
    chunk = span * 2 * rows
    left = lax.broadcasted_iota(jnp.int32, (chunk, 2 * HEAD_DIM), 1) < HEAD_DIM
    key_lane = lax.broadcasted_iota(jnp.int32, (chunk, PAGE), 1)
    row_index = lax.broadcasted_iota(jnp.int32, (chunk, PAGE), 0)

    def pair_copy(step):
        return pltpu.make_async_remote_copy(
            src_ref=parts_out.at[step, 1],
            dst_ref=pair_in.at[step],
            send_sem=pair_send.at[step],
            recv_sem=pair_recv.at[step],
            device_id=device(0, 1),
            device_id_type=MESH,
        )

    def part_copy(step):
        back = (CHIPS - step) % CHIPS
        return pltpu.make_async_remote_copy(
            src_ref=merged.at[step],
            dst_ref=parts_in.at[back],
            send_sem=part_send.at[step],
            recv_sem=part_recv.at[back],
            device_id=device(step, 0),
            device_id_type=MESH,
        )

    def last_copy(step, other):
        back = CHIPS - step
        return pltpu.make_async_remote_copy(
            src_ref=parts_out.at[step, other],
            dst_ref=last_in.at[back // (CHIPS - 1), other],
            send_sem=last_send.at[step // (CHIPS - 1), other],
            recv_sem=last_recv.at[back // (CHIPS - 1), other],
            device_id=device(step, other),
            device_id_type=MESH,
        )

    last_blocks = [(step, other) for step in (1, CHIPS - 1) for other in (0, 1)]

    def steps_of(index):
        later = (index + 3) // 4
        return [later * (4 - index * (index - 1) // 2), 2 + later * (2 + index)]

    def join_pair(index):
        steps = steps_of(index)
        for step in steps:
            pair_copy(step).wait_recv()
        mine = jnp.concatenate([parts_out[step, 0] for step in steps], axis=0)
        partner = jnp.concatenate([pair_in[step] for step in steps], axis=0)
        factors, logs = merge_weights(
            [read_logs(mine[:, width:]), read_logs(partner[:, width:])], spread[...], heads
        )
        half = span * rows
        both = factors[:half] * mine[:, :width].astype(jnp.float32) + factors[
            half:
        ] * partner[:, :width].astype(jnp.float32)
        both = both.astype(jnp.bfloat16)
        stat = write_logs(logs, heads)
        for i, step in enumerate(steps):
            here = slice(i * rows, (i + 1) * rows)
            merged[step, :, pl.ds(0, width)] = both[here]
            merged[step, :, pl.ds(width, PAGE)] = stat[here]
        for step in steps:

            @pl.when(step > 0)
            def _():
                part_copy(step).start()

    def attend(index, between):
        steps = steps_of(index)
        fresh = None
        for i, step in enumerate(steps):
            for other in (0, 1):
                first = (2 * i + other) * rows
                offset = row_index - first
                inside = (offset >= 0) & (offset < rows)
                later = jnp.where(
                    step == 0, jnp.where(core + other == 1, 1 - core, 0), (chip + step < CHIPS) * 1
                )
                own = jnp.where(step == 0, 1 - other, 0)
                limit = jnp.where(own == 1, offset, jnp.where(later == 1, rows, -1))
                fresh = jnp.where(inside, limit, 0 if fresh is None else fresh)
        visible = key_lane <= fresh
        packed = jnp.zeros((chunk, PAGE), jnp.float32)

        def columns(pair):
            return slice(pair * 2 * HEAD_DIM, (pair + 1) * 2 * HEAD_DIM)

        def scores_of(head):
            at = columns(head // 2)
            q = jnp.concatenate(
                [queries[step, other, :, at] for step in steps for other in (0, 1)], axis=0
            )
            q = q * jnp.asarray(HEAD_DIM**-0.5, q.dtype)
            zero = jnp.zeros_like(q)
            q = jnp.where(left, zero, q) if head % 2 else jnp.where(left, q, zero)
            return lax.dot_general(
                q, keys[:, at], (((1,), (1,)), ((), ())), preferred_element_type=jnp.float32
            )

        def weigh(head, scores):
            cost = costs[pl.ds(head, 1), :]
            old = scores[:, :slots] - cost[:, :slots]
            new = jnp.where(visible, scores[:, slots:] - cost[:, slots:], -DEAD)
            highest = jnp.maximum(
                jnp.max(old, axis=1, keepdims=True), jnp.max(new, axis=1, keepdims=True)
            )
            weights = jnp.concatenate(
                [
                    jnp.exp(old - highest).astype(jnp.bfloat16),
                    jnp.exp(new - highest).astype(jnp.bfloat16),
                ],
                axis=1,
            )
            value_pair = jnp.concatenate(
                [
                    values[:, columns(head // 2)],
                    jnp.ones((all_keys, 2 * HEAD_DIM), values.dtype),
                ],
                axis=1,
            )
            summed = jnp.dot(weights, value_pair, preferred_element_type=jnp.float32)
            sums = summed[:, 2 * HEAD_DIM :]
            return summed[:, : 2 * HEAD_DIM] / sums, highest + jnp.log(sums)

        ahead = scores_of(0)
        for pair in range(pairs):
            at = columns(pair)
            both = []
            for head in (2 * pair, 2 * pair + 1):
                if head == BETWEEN:
                    between()
                scores = ahead
                ahead = scores_of(head + 1) if head + 1 < heads else None
                mean, log = weigh(head, scores)
                both.append(mean)
                packed = jnp.where(key_lane == head, log, packed)
            out = jnp.where(left, both[0], both[1]).astype(jnp.bfloat16)
            for i in range(2 * span):
                parts_out[steps[i // 2], i % 2, :, at] = out[i * rows : (i + 1) * rows]
        stat = write_logs(packed, heads)
        for i in range(2 * span):
            parts_out[steps[i // 2], i % 2, :, pl.ds(width, PAGE)] = stat[
                i * rows : (i + 1) * rows
            ]

        @pl.when(index < turns - 1)
        def _():
            for step in steps:
                pair_copy(step).start()

    turns = CHIPS // span

    def turn(index, _):
        @pl.when(index > 0)
        def _():
            for step in steps_of(index):
                query_relay(step).wait_recv()

        def between():
            @pl.when(index < turns - 1)
            def _():
                for step in steps_of(index + 1):
                    query_direct(CHIPS - step, 0).wait_recv()
                    query_relay(step).start()

            @pl.when(index > 0)
            def _():
                join_pair(index - 1)

        attend(index, between)
        return 0

    lax.fori_loop(0, turns, turn, 0)
    for step, other in last_blocks:
        last_copy(step, other).start()

    middle_steps = range(2, CHIPS - 1)
    for step in middle_steps:
        part_copy(CHIPS - step).wait_recv()
    for step, other in last_blocks:
        last_copy(CHIPS - step, other).wait_recv()
    parts = [merged.at[0]] + [parts_in.at[step] for step in middle_steps]
    parts += [last_in.at[side, other] for side in (0, 1) for other in (0, 1)]
    factors, _ = merge_weights(
        [read_logs(part[:, pl.ds(width, PAGE)]) for part in parts], spread[...], heads
    )
    attention = jnp.zeros((rows, width), jnp.float32)
    for i, part in enumerate(parts):
        attention = attention + factors[i * rows : (i + 1) * rows] * part[
            :, pl.ds(0, width)
        ].astype(jnp.float32)
    attention = attention.astype(jnp.bfloat16)

    def share_copy(step):
        return pltpu.make_async_remote_copy(
            src_ref=shares_out.at[step - 1],
            dst_ref=shares_in.at[tp_count - step - 1],
            send_sem=share_send.at[step - 1],
            recv_sem=share_recv.at[tp_count - step - 1],
            device_id=(seq, (tp + step) % tp_count),
            device_id_type=MESH,
        )

    def share(step):
        block = (tp + step) % tp_count
        columns = pl.ds(pl.multiple_of(block * width, PAGE), width)
        return jnp.dot(attention, weight[:, columns], preferred_element_type=jnp.float32)

    for step in (2, 1, 3)[: tp_count - 1]:
        shares_out[step - 1] = share(step).astype(jnp.bfloat16)
        share_copy(step).start()
    summed = share(0) + residual_ref[...].astype(jnp.float32)
    for step in range(1, tp_count):
        share_copy(step).wait_recv()
        summed = summed + shares_in[tp_count - step - 1].astype(jnp.float32)
    out_ref[...] = summed.astype(out_ref.dtype)

    for step, other in first_sends + later_sends:
        query_direct(step, other).wait_send()
    for step in (1, 3, 4, 5, 6, 7):
        query_relay(step).wait_send()
    for step, other in peers:
        forget_copy(step, other).wait_send()
    pair_copy(0).wait_send()
    for step in middle_steps:
        pair_copy(step).wait_send()
        part_copy(step).wait_send()
    for step, other in last_blocks:
        last_copy(step, other).wait_send()
    for step in range(1, tp_count):
        share_copy(step).wait_send()


def shards(
    queries,
    new_keys,
    new_values,
    forget_logit,
    cache_keys,
    cache_values,
    cache_decay,
    slot_page,
    cache_len,
    residual,
    out_weight,
):
    rows, width = queries.shape
    heads = forget_logit.shape[0]
    slots = cache_keys.shape[0]
    tp_count = lax.axis_size("tp")
    vmem = pl.BlockSpec(memory_space=pltpu.VMEM)
    smem = pl.BlockSpec(memory_space=pltpu.SMEM)
    anywhere = pl.BlockSpec(memory_space=pl.ANY)
    dma = pltpu.SemaphoreType.DMA
    half = jnp.bfloat16
    single = jnp.float32
    return pl.pallas_call(
        functools.partial(layer_kernel, tp_count),
        out_shape=(
            jax.ShapeDtypeStruct((rows, width), half),
            jax.ShapeDtypeStruct((heads, rows), single),
        ),
        in_specs=[
            anywhere, anywhere, anywhere, anywhere, anywhere, anywhere, anywhere, smem, smem,
            anywhere, anywhere,
        ],
        out_specs=(vmem, vmem),
        scratch_shapes=[
            pltpu.VMEM((slots + PAGE, width), half),
            pltpu.VMEM((slots + PAGE, width), half),
            pltpu.VMEM(out_weight.shape, half),
            pltpu.VMEM(forget_logit.shape, single),
            pltpu.VMEM(cache_decay.shape, single),
            pltpu.VMEM(residual.shape, half),
            pltpu.VMEM((8, slots + PAGE), single),
            pltpu.VMEM((CHIPS, 2, rows, width), half),
            pltpu.VMEM((8, PAGE), single),
            pltpu.VMEM((1, PAGE), single),
            pltpu.VMEM((CHIPS, 2, 1, PAGE), single),
            pltpu.VMEM((2 * PAGE, width), half),
            pltpu.VMEM((CHIPS, 2, rows, width + PAGE), half),
            pltpu.VMEM((CHIPS, rows, width + PAGE), half),
            pltpu.VMEM((CHIPS, rows, width + PAGE), half),
            pltpu.VMEM((CHIPS, rows, width + PAGE), half),
            pltpu.VMEM((2, 2, rows, width + PAGE), half),
            pltpu.VMEM((max(tp_count - 1, 1), rows, width), half),
            pltpu.VMEM((max(tp_count - 1, 1), rows, width), half),
            dma((9,)),
            dma((CHIPS, 2)),
            dma((CHIPS, 2)),
            dma((CHIPS, 2)),
            dma((CHIPS, 2)),
            dma((CHIPS,)),
            dma((CHIPS,)),
            dma((CHIPS,)),
            dma((CHIPS,)),
            dma((2, 2)),
            dma((2, 2)),
            dma((max(tp_count - 1, 1),)),
            dma((max(tp_count - 1, 1),)),
        ],
        compiler_params=pltpu.CompilerParams(
            collective_id=0, has_side_effects=True, vmem_limit_bytes=60 * 1024 * 1024
        ),
        name="layer",
    )(
        queries, new_keys, new_values, forget_logit, cache_keys, cache_values, cache_decay,
        slot_page, cache_len, residual, out_weight,
    )


def solution(mesh):
    return jax.shard_map(
        shards,
        mesh=mesh,
        in_specs=(
            P("seq", "tp"),
            P("seq", "tp"),
            P("seq", "tp"),
            P("tp", "seq"),
            P("seq", "tp"),
            P("seq", "tp"),
            P("tp", "seq"),
            P("seq"),
            P(),
            P("seq", "tp"),
            P("tp", None),
        ),
        out_specs=(P("seq", "tp"), P("tp", "seq")),
        check_vma=False,
    )
```

```python
import functools

import jax
import jax.numpy as jnp
from jax import lax
from jax.experimental import pallas as pl
from jax.experimental.pallas import tpu as pltpu
from jax.sharding import PartitionSpec as P

HEAD_DIM = 64
PAGE = 128
CHIPS = 8
GROUP = 16
DEAD = 1e30
BETWEEN = 4
MESH = pl.DeviceIdType.MESH


def thirds(x):
    high = x.astype(jnp.bfloat16)
    rest = x - high.astype(jnp.float32)
    middle = rest.astype(jnp.bfloat16)
    low = (rest - middle.astype(jnp.float32)).astype(jnp.bfloat16)
    return high, middle, low


def merge_weights(logs, spread, heads):
    top = functools.reduce(jnp.maximum, logs)
    shares = [jnp.exp(log - top) for log in logs]
    whole = functools.reduce(jnp.add, shares)
    stacked = jnp.concatenate([share / whole for share in shares], axis=0)
    lane = lax.broadcasted_iota(jnp.int32, stacked.shape, 1)
    stacked = jnp.where(lane < heads, stacked, 0.0)
    high, middle, _ = thirds(stacked)
    factors = jnp.dot(
        jnp.concatenate([high, middle], axis=1), spread, preferred_element_type=jnp.float32
    )
    return factors, top + jnp.log(whole)


def read_logs(stat):
    stat = stat.astype(jnp.float32)
    return stat + pltpu.roll(stat, PAGE - 8, 1) + pltpu.roll(stat, PAGE - 16, 1)


def write_logs(logs, heads):
    lane = lax.broadcasted_iota(jnp.int32, logs.shape, 1)
    high, middle, low = (
        part.astype(jnp.float32) for part in thirds(jnp.where(lane < heads, logs, 0.0))
    )
    packed = high + pltpu.roll(middle, 8, 1) + pltpu.roll(low, 16, 1)
    return packed.astype(jnp.bfloat16)


def layer_kernel(
    tp_count,
    q_ref,
    new_keys,
    new_values,
    logit_in,
    cache_keys,
    cache_values,
    decay_in,
    page_ref,
    length_ref,
    residual_in,
    out_weight,
    out_ref,
    forget_ref,
    keys,
    values,
    weight,
    logit_ref,
    decay_ref,
    residual_ref,
    costs,
    queries,
    forget_tile,
    forget_row,
    forget_all,
    spread,
    parts_out,
    pair_in,
    merged,
    parts_in,
    shares_out,
    shares_in,
    local_sem,
    query_send,
    query_recv,
    forget_send,
    forget_recv,
    pair_send,
    pair_recv,
    part_send,
    part_recv,
    share_send,
    share_recv,
):
    rows, width = q_ref.shape
    heads = width // HEAD_DIM
    pairs = heads // 2
    slots = cache_keys.shape[0]
    all_keys = keys.shape[0]
    seq = lax.axis_index("seq")
    tp = lax.axis_index("tp")
    request = seq // GROUP
    chip = (seq % GROUP) // 2
    core = seq % 2

    def device(chip_step, other):
        there = (chip + chip_step) % CHIPS
        return (request * GROUP + there * 2 + (1 - core if other else core), tp)

    barrier = pltpu.get_barrier_semaphore()
    peers = [(step, other) for step in range(CHIPS) for other in (0, 1) if step or other]
    for step, other in peers:
        pl.semaphore_signal(barrier, inc=1, device_id=device(step, other), device_id_type=MESH)
    for step in range(1, tp_count):
        pl.semaphore_signal(
            barrier, inc=1, device_id=(seq, (tp + step) % tp_count), device_id_type=MESH
        )

    local = [
        pltpu.make_async_copy(source, target, local_sem.at[i])
        for i, (source, target) in enumerate(
            [
                (logit_in, logit_ref),
                (q_ref, queries.at[0, 0]),
                (decay_in, decay_ref),
                (new_keys, keys.at[pl.ds(slots, rows)]),
                (new_values, values.at[pl.ds(slots, rows)]),
                (cache_keys, keys.at[pl.ds(0, slots)]),
                (cache_values, values.at[pl.ds(0, slots)]),
                (out_weight, weight),
                (residual_in, residual_ref),
            ]
        )
    ]
    for copy in local:
        copy.start()

    pad = all_keys - slots - rows
    keys[pl.ds(slots + rows, pad), :] = jnp.zeros((pad, width), keys.dtype)
    values[pl.ds(slots + rows, pad), :] = jnp.zeros((pad, width), values.dtype)
    forget_tile[...] = jnp.zeros(forget_tile.shape, jnp.float32)
    spread_row = lax.broadcasted_iota(jnp.int32, spread.shape, 0) % PAGE
    spread_lane = lax.broadcasted_iota(jnp.int32, spread.shape, 1) // HEAD_DIM
    spread[...] = jnp.where(spread_row == spread_lane, 1.0, 0.0).astype(spread.dtype)
    local[0].wait()
    logit = logit_ref[...]
    forget_tile[pl.ds(0, heads), pl.ds(0, rows)] = -jnp.log1p(jnp.exp(-logit))
    lane = lax.broadcasted_iota(jnp.int32, forget_tile.shape, 1)
    running = forget_tile[...]
    reach = 1
    while reach < rows:
        running = running + jnp.where(lane >= reach, pltpu.roll(running, reach, 1), 0.0)
        reach *= 2
    total = jnp.sum(jnp.where(lane == rows - 1, running, 0.0), axis=1, keepdims=True)
    head_row = lax.broadcasted_iota(jnp.int32, forget_tile.shape, 0)
    forget_row[...] = jnp.sum(jnp.where(head_row == lane, total, 0.0), axis=0, keepdims=True)
    pl.semaphore_wait(barrier, len(peers) + tp_count - 1)

    def query_direct(step, other):
        back = (CHIPS - step) % CHIPS
        return pltpu.make_async_remote_copy(
            src_ref=q_ref,
            dst_ref=queries.at[back, other],
            send_sem=query_send.at[step, other],
            recv_sem=query_recv.at[back, other],
            device_id=device(step, other),
            device_id_type=MESH,
        )

    def query_relay(step):
        return pltpu.make_async_remote_copy(
            src_ref=queries.at[step, 0],
            dst_ref=queries.at[step, 1],
            send_sem=query_send.at[8 - step, 1],
            recv_sem=query_recv.at[step, 1],
            device_id=device(0, 1),
            device_id_type=MESH,
        )

    def forget_copy(step, other):
        return pltpu.make_async_remote_copy(
            src_ref=forget_row,
            dst_ref=forget_all.at[(CHIPS - step) % CHIPS, other],
            send_sem=forget_send.at[step, other],
            recv_sem=forget_recv.at[(CHIPS - step) % CHIPS, other],
            device_id=device(step, other),
            device_id_type=MESH,
        )

    for step, other in peers:
        forget_copy(step, other).start()
    first_sends = [(0, 1), (6, 0), (6, 1)]
    later_sends = [(step, 0) for step in (4, 3, 5, 2, 7, 1)]
    for step, other in first_sends + later_sends:
        query_direct(step, other).start()

    local[2].wait()
    length = length_ref[request]
    page_lane = lax.broadcasted_iota(jnp.int32, (1, PAGE), 1)
    for page in range(slots // PAGE):
        alive = page_ref[page] * PAGE + page_lane < length
        at = pl.ds(page * PAGE, PAGE)
        costs[pl.ds(0, heads), at] = jnp.where(alive, decay_ref[:, at], DEAD)
    for i in (1, 3, 4, 5, 6, 7, 8):
        local[i].wait()

    for step, other in peers:
        forget_copy((CHIPS - step) % CHIPS, other).wait_recv()
    before = jnp.zeros(forget_row.shape, jnp.float32)
    for step, other in peers:
        earlier = (core == 1) if step == 0 else (chip + step >= CHIPS)
        before = before + jnp.where(earlier, forget_all[step, other], 0.0)
    own_forget = running + jnp.sum(
        jnp.where(head_row == lane, before, 0.0), axis=1, keepdims=True
    )
    forget_ref[...] = own_forget[:heads, :rows]
    costs[:, pl.ds(slots, PAGE)] = jnp.where(lane < rows, own_forget, DEAD)
    for step, other in first_sends:
        query_direct(step, other).wait_recv()

    span = 2
    chunk = span * 2 * rows
    left = lax.broadcasted_iota(jnp.int32, (chunk, 2 * HEAD_DIM), 1) < HEAD_DIM
    key_lane = lax.broadcasted_iota(jnp.int32, (chunk, PAGE), 1)
    row_index = lax.broadcasted_iota(jnp.int32, (chunk, PAGE), 0)

    def pair_copy(step):
        return pltpu.make_async_remote_copy(
            src_ref=parts_out.at[step, 1],
            dst_ref=pair_in.at[step],
            send_sem=pair_send.at[step],
            recv_sem=pair_recv.at[step],
            device_id=device(0, 1),
            device_id_type=MESH,
        )

    def part_copy(step):
        back = (CHIPS - step) % CHIPS
        return pltpu.make_async_remote_copy(
            src_ref=merged.at[step],
            dst_ref=parts_in.at[back],
            send_sem=part_send.at[step],
            recv_sem=part_recv.at[back],
            device_id=device(step, 0),
            device_id_type=MESH,
        )

    def steps_of(index):
        later = (index + 3) // 4
        return [later * (4 - index * (index - 1) // 2), 2 + later * (2 + index)]

    def join_pair(index):
        steps = steps_of(index)
        for step in steps:
            pair_copy(step).wait_recv()
        mine = jnp.concatenate([parts_out[step, 0] for step in steps], axis=0)
        partner = jnp.concatenate([pair_in[step] for step in steps], axis=0)
        factors, logs = merge_weights(
            [read_logs(mine[:, width:]), read_logs(partner[:, width:])], spread[...], heads
        )
        half = span * rows
        both = factors[:half] * mine[:, :width].astype(jnp.float32) + factors[
            half:
        ] * partner[:, :width].astype(jnp.float32)
        both = both.astype(jnp.bfloat16)
        stat = write_logs(logs, heads)
        for i, step in enumerate(steps):
            here = slice(i * rows, (i + 1) * rows)
            merged[step, :, pl.ds(0, width)] = both[here]
            merged[step, :, pl.ds(width, PAGE)] = stat[here]
        for step in steps:

            @pl.when(step > 0)
            def _():
                part_copy(step).start()

    def attend(index, between):
        steps = steps_of(index)
        fresh = None
        for i, step in enumerate(steps):
            for other in (0, 1):
                first = (2 * i + other) * rows
                offset = row_index - first
                inside = (offset >= 0) & (offset < rows)
                later = jnp.where(
                    step == 0, jnp.where(core + other == 1, 1 - core, 0), (chip + step < CHIPS) * 1
                )
                own = jnp.where(step == 0, 1 - other, 0)
                limit = jnp.where(own == 1, offset, jnp.where(later == 1, rows, -1))
                fresh = jnp.where(inside, limit, 0 if fresh is None else fresh)
        visible = key_lane <= fresh
        packed = jnp.zeros((chunk, PAGE), jnp.float32)

        def columns(pair):
            return slice(pair * 2 * HEAD_DIM, (pair + 1) * 2 * HEAD_DIM)

        def scores_of(pair):
            at = columns(pair)
            q = jnp.concatenate(
                [queries[step, other, :, at] for step in steps for other in (0, 1)], axis=0
            )
            q = q * jnp.asarray(HEAD_DIM**-0.5, q.dtype)
            zero = jnp.zeros_like(q)
            q = jnp.concatenate(
                [jnp.where(left, q, zero), jnp.where(left, zero, q)], axis=0
            )
            return lax.dot_general(
                q, keys[:, at], (((1,), (1,)), ((), ())), preferred_element_type=jnp.float32
            )

        def weigh(head, scores):
            cost = costs[pl.ds(head, 1), :]
            old = scores[:, :slots] - cost[:, :slots]
            new = jnp.where(visible, scores[:, slots:] - cost[:, slots:], -DEAD)
            highest = jnp.maximum(
                jnp.max(old, axis=1, keepdims=True), jnp.max(new, axis=1, keepdims=True)
            )
            weights = jnp.concatenate(
                [
                    jnp.exp(old - highest).astype(jnp.bfloat16),
                    jnp.exp(new - highest).astype(jnp.bfloat16),
                ],
                axis=1,
            )
            value_pair = jnp.concatenate(
                [
                    values[:, columns(head // 2)],
                    jnp.ones((all_keys, 2 * HEAD_DIM), values.dtype),
                ],
                axis=1,
            )
            summed = jnp.dot(weights, value_pair, preferred_element_type=jnp.float32)
            sums = summed[:, 2 * HEAD_DIM :]
            return summed[:, : 2 * HEAD_DIM] / sums, highest + jnp.log(sums)

        ahead = scores_of(0)
        for pair in range(pairs):
            at = columns(pair)
            both = []
            for head in (2 * pair, 2 * pair + 1):
                if head == BETWEEN:
                    between()
                if head % 2 == 0:
                    pair_scores = ahead
                    ahead = scores_of(pair + 1) if pair + 1 < pairs else None
                first = head % 2 * chunk
                scores = pair_scores[first : first + chunk]
                mean, log = weigh(head, scores)
                both.append(mean)
                packed = jnp.where(key_lane == head, log, packed)
            out = jnp.where(left, both[0], both[1]).astype(jnp.bfloat16)
            for i in range(2 * span):
                parts_out[steps[i // 2], i % 2, :, at] = out[i * rows : (i + 1) * rows]
        stat = write_logs(packed, heads)
        for i in range(2 * span):
            parts_out[steps[i // 2], i % 2, :, pl.ds(width, PAGE)] = stat[
                i * rows : (i + 1) * rows
            ]
        for step in steps:
            pair_copy(step).start()

    turns = CHIPS // span

    def turn(index, _):
        @pl.when(index > 0)
        def _():
            for step in steps_of(index):
                query_relay(step).wait_recv()

        def between():
            @pl.when(index < turns - 1)
            def _():
                for step in steps_of(index + 1):
                    query_direct(CHIPS - step, 0).wait_recv()
                    query_relay(step).start()

            @pl.when(index > 0)
            def _():
                join_pair(index - 1)

        attend(index, between)
        return 0

    lax.fori_loop(0, turns, turn, 0)
    join_pair(turns - 1)

    for step in range(1, CHIPS):
        part_copy(CHIPS - step).wait_recv()

    def part(step, at):
        return parts_in[step, :, at] if step else merged[0, :, at]

    factors, _ = merge_weights(
        [read_logs(part(step, pl.ds(width, PAGE))) for step in range(CHIPS)], spread[...], heads
    )
    attention = jnp.zeros((rows, width), jnp.float32)
    for step in range(CHIPS):
        attention = attention + factors[step * rows : (step + 1) * rows] * part(
            step, pl.ds(0, width)
        ).astype(jnp.float32)
    attention = attention.astype(jnp.bfloat16)

    def share_copy(step):
        return pltpu.make_async_remote_copy(
            src_ref=shares_out.at[step - 1],
            dst_ref=shares_in.at[tp_count - step - 1],
            send_sem=share_send.at[step - 1],
            recv_sem=share_recv.at[tp_count - step - 1],
            device_id=(seq, (tp + step) % tp_count),
            device_id_type=MESH,
        )

    def share(step):
        block = (tp + step) % tp_count
        columns = pl.ds(pl.multiple_of(block * width, PAGE), width)
        return jnp.dot(attention, weight[:, columns], preferred_element_type=jnp.float32)

    for step in (2, 1, 3)[: tp_count - 1]:
        shares_out[step - 1] = share(step).astype(jnp.bfloat16)
        share_copy(step).start()
    summed = share(0) + residual_ref[...].astype(jnp.float32)
    for step in range(1, tp_count):
        share_copy(step).wait_recv()
        summed = summed + shares_in[tp_count - step - 1].astype(jnp.float32)
    out_ref[...] = summed.astype(out_ref.dtype)

    for step, other in first_sends + later_sends:
        query_direct(step, other).wait_send()
    for step in (1, 3, 4, 5, 6, 7):
        query_relay(step).wait_send()
    for step, other in peers:
        forget_copy(step, other).wait_send()
    for step in range(CHIPS):
        pair_copy(step).wait_send()
        if step:
            part_copy(step).wait_send()
    for step in range(1, tp_count):
        share_copy(step).wait_send()


def shards(
    queries,
    new_keys,
    new_values,
    forget_logit,
    cache_keys,
    cache_values,
    cache_decay,
    slot_page,
    cache_len,
    residual,
    out_weight,
):
    rows, width = queries.shape
    heads = forget_logit.shape[0]
    slots = cache_keys.shape[0]
    tp_count = lax.axis_size("tp")
    vmem = pl.BlockSpec(memory_space=pltpu.VMEM)
    smem = pl.BlockSpec(memory_space=pltpu.SMEM)
    anywhere = pl.BlockSpec(memory_space=pl.ANY)
    dma = pltpu.SemaphoreType.DMA
    half = jnp.bfloat16
    single = jnp.float32
    return pl.pallas_call(
        functools.partial(layer_kernel, tp_count),
        out_shape=(
            jax.ShapeDtypeStruct((rows, width), half),
            jax.ShapeDtypeStruct((heads, rows), single),
        ),
        in_specs=[
            anywhere, anywhere, anywhere, anywhere, anywhere, anywhere, anywhere, smem, smem,
            anywhere, anywhere,
        ],
        out_specs=(vmem, vmem),
        scratch_shapes=[
            pltpu.VMEM((slots + PAGE, width), half),
            pltpu.VMEM((slots + PAGE, width), half),
            pltpu.VMEM(out_weight.shape, half),
            pltpu.VMEM(forget_logit.shape, single),
            pltpu.VMEM(cache_decay.shape, single),
            pltpu.VMEM(residual.shape, half),
            pltpu.VMEM((8, slots + PAGE), single),
            pltpu.VMEM((CHIPS, 2, rows, width), half),
            pltpu.VMEM((8, PAGE), single),
            pltpu.VMEM((1, PAGE), single),
            pltpu.VMEM((CHIPS, 2, 1, PAGE), single),
            pltpu.VMEM((2 * PAGE, width), half),
            pltpu.VMEM((CHIPS, 2, rows, width + PAGE), half),
            pltpu.VMEM((CHIPS, rows, width + PAGE), half),
            pltpu.VMEM((CHIPS, rows, width + PAGE), half),
            pltpu.VMEM((CHIPS, rows, width + PAGE), half),
            pltpu.VMEM((max(tp_count - 1, 1), rows, width), half),
            pltpu.VMEM((max(tp_count - 1, 1), rows, width), half),
            dma((9,)),
            dma((CHIPS, 2)),
            dma((CHIPS, 2)),
            dma((CHIPS, 2)),
            dma((CHIPS, 2)),
            dma((CHIPS,)),
            dma((CHIPS,)),
            dma((CHIPS,)),
            dma((CHIPS,)),
            dma((max(tp_count - 1, 1),)),
            dma((max(tp_count - 1, 1),)),
        ],
        compiler_params=pltpu.CompilerParams(
            collective_id=0, has_side_effects=True, vmem_limit_bytes=60 * 1024 * 1024
        ),
        name="layer",
    )(
        queries, new_keys, new_values, forget_logit, cache_keys, cache_values, cache_decay,
        slot_page, cache_len, residual, out_weight,
    )


def solution(mesh):
    return jax.shard_map(
        shards,
        mesh=mesh,
        in_specs=(
            P("seq", "tp"),
            P("seq", "tp"),
            P("seq", "tp"),
            P("tp", "seq"),
            P("seq", "tp"),
            P("seq", "tp"),
            P("tp", "seq"),
            P("seq"),
            P(),
            P("seq", "tp"),
            P("tp", None),
        ),
        out_specs=(P("seq", "tp"), P("tp", "seq")),
        check_vma=False,
    )
```

```python
import functools

import jax
import jax.numpy as jnp
from jax import lax
from jax.experimental import pallas as pl
from jax.experimental.pallas import tpu as pltpu
from jax.sharding import PartitionSpec as P

HEAD_DIM = 64
PAGE = 128
CHIPS = 8
GROUP = 16
DEAD = 1e30
BETWEEN = 2
MESH = pl.DeviceIdType.MESH


def thirds(x):
    high = x.astype(jnp.bfloat16)
    rest = x - high.astype(jnp.float32)
    middle = rest.astype(jnp.bfloat16)
    low = (rest - middle.astype(jnp.float32)).astype(jnp.bfloat16)
    return high, middle, low


def merge_weights(logs, spread, heads):
    top = functools.reduce(jnp.maximum, logs)
    shares = [jnp.exp(log - top) for log in logs]
    whole = functools.reduce(jnp.add, shares)
    stacked = jnp.concatenate([share / whole for share in shares], axis=0)
    lane = lax.broadcasted_iota(jnp.int32, stacked.shape, 1)
    stacked = jnp.where(lane < heads, stacked, 0.0)
    high, middle, _ = thirds(stacked)
    factors = jnp.dot(
        jnp.concatenate([high, middle], axis=1), spread, preferred_element_type=jnp.float32
    )
    return factors, top + jnp.log(whole)


def read_logs(stat):
    stat = stat.astype(jnp.float32)
    return stat + pltpu.roll(stat, PAGE - 8, 1) + pltpu.roll(stat, PAGE - 16, 1)


def write_logs(logs, heads):
    lane = lax.broadcasted_iota(jnp.int32, logs.shape, 1)
    high, middle, low = (
        part.astype(jnp.float32) for part in thirds(jnp.where(lane < heads, logs, 0.0))
    )
    packed = high + pltpu.roll(middle, 8, 1) + pltpu.roll(low, 16, 1)
    return packed.astype(jnp.bfloat16)


def layer_kernel(
    tp_count,
    q_ref,
    new_keys,
    new_values,
    logit_in,
    cache_keys,
    cache_values,
    decay_in,
    page_ref,
    length_ref,
    residual_in,
    out_weight,
    out_ref,
    forget_ref,
    keys,
    values,
    weight,
    logit_ref,
    decay_ref,
    residual_ref,
    costs,
    queries,
    forget_tile,
    forget_row,
    forget_all,
    spread,
    parts_out,
    pair_in,
    merged,
    parts_in,
    shares_out,
    shares_in,
    local_sem,
    query_send,
    query_recv,
    forget_send,
    forget_recv,
    pair_send,
    pair_recv,
    part_send,
    part_recv,
    share_send,
    share_recv,
):
    rows, width = q_ref.shape
    heads = width // HEAD_DIM
    pairs = heads // 2
    slots = cache_keys.shape[0]
    all_keys = keys.shape[0]
    seq = lax.axis_index("seq")
    tp = lax.axis_index("tp")
    request = seq // GROUP
    chip = (seq % GROUP) // 2
    core = seq % 2

    def device(chip_step, other):
        there = (chip + chip_step) % CHIPS
        return (request * GROUP + there * 2 + (1 - core if other else core), tp)

    barrier = pltpu.get_barrier_semaphore()
    peers = [(step, other) for step in range(CHIPS) for other in (0, 1) if step or other]
    for step, other in peers:
        pl.semaphore_signal(barrier, inc=1, device_id=device(step, other), device_id_type=MESH)
    for step in range(1, tp_count):
        pl.semaphore_signal(
            barrier, inc=1, device_id=(seq, (tp + step) % tp_count), device_id_type=MESH
        )

    local = [
        pltpu.make_async_copy(source, target, local_sem.at[i])
        for i, (source, target) in enumerate(
            [
                (logit_in, logit_ref),
                (q_ref, queries.at[0, 0]),
                (decay_in, decay_ref),
                (new_keys, keys.at[pl.ds(slots, rows)]),
                (new_values, values.at[pl.ds(slots, rows)]),
                (cache_keys, keys.at[pl.ds(0, slots)]),
                (cache_values, values.at[pl.ds(0, slots)]),
                (out_weight, weight),
                (residual_in, residual_ref),
            ]
        )
    ]
    for copy in local:
        copy.start()

    pad = all_keys - slots - rows
    keys[pl.ds(slots + rows, pad), :] = jnp.zeros((pad, width), keys.dtype)
    values[pl.ds(slots + rows, pad), :] = jnp.zeros((pad, width), values.dtype)
    forget_tile[...] = jnp.zeros(forget_tile.shape, jnp.float32)
    spread_row = lax.broadcasted_iota(jnp.int32, spread.shape, 0) % PAGE
    spread_lane = lax.broadcasted_iota(jnp.int32, spread.shape, 1) // HEAD_DIM
    spread[...] = jnp.where(spread_row == spread_lane, 1.0, 0.0).astype(spread.dtype)
    local[0].wait()
    logit = logit_ref[...]
    forget_tile[pl.ds(0, heads), pl.ds(0, rows)] = -jnp.log1p(jnp.exp(-logit))
    lane = lax.broadcasted_iota(jnp.int32, forget_tile.shape, 1)
    running = forget_tile[...]
    reach = 1
    while reach < rows:
        running = running + jnp.where(lane >= reach, pltpu.roll(running, reach, 1), 0.0)
        reach *= 2
    total = jnp.sum(jnp.where(lane == rows - 1, running, 0.0), axis=1, keepdims=True)
    head_row = lax.broadcasted_iota(jnp.int32, forget_tile.shape, 0)
    forget_row[...] = jnp.sum(jnp.where(head_row == lane, total, 0.0), axis=0, keepdims=True)
    pl.semaphore_wait(barrier, len(peers) + tp_count - 1)

    def query_direct(step, other):
        back = (CHIPS - step) % CHIPS
        return pltpu.make_async_remote_copy(
            src_ref=q_ref,
            dst_ref=queries.at[back, other],
            send_sem=query_send.at[step, other],
            recv_sem=query_recv.at[back, other],
            device_id=device(step, other),
            device_id_type=MESH,
        )

    def query_relay(step):
        return pltpu.make_async_remote_copy(
            src_ref=queries.at[step, 0],
            dst_ref=queries.at[step, 1],
            send_sem=query_send.at[8 - step, 1],
            recv_sem=query_recv.at[step, 1],
            device_id=device(0, 1),
            device_id_type=MESH,
        )

    def forget_copy(step, other):
        return pltpu.make_async_remote_copy(
            src_ref=forget_row,
            dst_ref=forget_all.at[(CHIPS - step) % CHIPS, other],
            send_sem=forget_send.at[step, other],
            recv_sem=forget_recv.at[(CHIPS - step) % CHIPS, other],
            device_id=device(step, other),
            device_id_type=MESH,
        )

    for step, other in peers:
        forget_copy(step, other).start()
    first_sends = [(0, 1), (6, 0), (6, 1)]
    later_sends = [(step, 0) for step in (4, 3, 5, 2, 7, 1)]
    for step, other in first_sends + later_sends:
        query_direct(step, other).start()

    local[2].wait()
    length = length_ref[request]
    page_lane = lax.broadcasted_iota(jnp.int32, (1, PAGE), 1)
    for page in range(slots // PAGE):
        alive = page_ref[page] * PAGE + page_lane < length
        at = pl.ds(page * PAGE, PAGE)
        costs[pl.ds(0, heads), at] = jnp.where(alive, decay_ref[:, at], DEAD)
    for i in (1, 3, 4, 5, 6, 7, 8):
        local[i].wait()

    for step, other in peers:
        forget_copy((CHIPS - step) % CHIPS, other).wait_recv()
    before = jnp.zeros(forget_row.shape, jnp.float32)
    for step, other in peers:
        earlier = (core == 1) if step == 0 else (chip + step >= CHIPS)
        before = before + jnp.where(earlier, forget_all[step, other], 0.0)
    own_forget = running + jnp.sum(
        jnp.where(head_row == lane, before, 0.0), axis=1, keepdims=True
    )
    forget_ref[...] = own_forget[:heads, :rows]
    costs[:, pl.ds(slots, PAGE)] = jnp.where(lane < rows, own_forget, DEAD)
    for step, other in first_sends:
        query_direct(step, other).wait_recv()

    span = 2
    chunk = span * 2 * rows
    left = lax.broadcasted_iota(jnp.int32, (chunk, 2 * HEAD_DIM), 1) < HEAD_DIM
    key_lane = lax.broadcasted_iota(jnp.int32, (chunk, PAGE), 1)
    row_index = lax.broadcasted_iota(jnp.int32, (chunk, PAGE), 0)

    def pair_copy(step):
        return pltpu.make_async_remote_copy(
            src_ref=parts_out.at[step, 1],
            dst_ref=pair_in.at[step],
            send_sem=pair_send.at[step],
            recv_sem=pair_recv.at[step],
            device_id=device(0, 1),
            device_id_type=MESH,
        )

    def part_copy(step):
        back = (CHIPS - step) % CHIPS
        return pltpu.make_async_remote_copy(
            src_ref=merged.at[step],
            dst_ref=parts_in.at[back],
            send_sem=part_send.at[step],
            recv_sem=part_recv.at[back],
            device_id=device(step, 0),
            device_id_type=MESH,
        )

    def steps_of(index):
        later = (index + 3) // 4
        return [later * (4 - index * (index - 1) // 2), 2 + later * (2 + index)]

    def join_pair(index):
        steps = steps_of(index)
        for step in steps:
            pair_copy(step).wait_recv()
        mine = jnp.concatenate([parts_out[step, 0] for step in steps], axis=0)
        partner = jnp.concatenate([pair_in[step] for step in steps], axis=0)
        factors, logs = merge_weights(
            [read_logs(mine[:, width:]), read_logs(partner[:, width:])], spread[...], heads
        )
        half = span * rows
        both = factors[:half] * mine[:, :width].astype(jnp.float32) + factors[
            half:
        ] * partner[:, :width].astype(jnp.float32)
        both = both.astype(jnp.bfloat16)
        stat = write_logs(logs, heads)
        for i, step in enumerate(steps):
            here = slice(i * rows, (i + 1) * rows)
            merged[step, :, pl.ds(0, width)] = both[here]
            merged[step, :, pl.ds(width, PAGE)] = stat[here]
        for step in steps:

            @pl.when(step > 0)
            def _():
                part_copy(step).start()

    def attend(index, between):
        steps = steps_of(index)
        fresh = None
        for i, step in enumerate(steps):
            for other in (0, 1):
                first = (2 * i + other) * rows
                offset = row_index - first
                inside = (offset >= 0) & (offset < rows)
                later = jnp.where(
                    step == 0, jnp.where(core + other == 1, 1 - core, 0), (chip + step < CHIPS) * 1
                )
                own = jnp.where(step == 0, 1 - other, 0)
                limit = jnp.where(own == 1, offset, jnp.where(later == 1, rows, -1))
                fresh = jnp.where(inside, limit, 0 if fresh is None else fresh)
        visible = key_lane <= fresh
        packed = jnp.zeros((chunk, PAGE), jnp.float32)

        def columns(pair):
            return slice(pair * 2 * HEAD_DIM, (pair + 1) * 2 * HEAD_DIM)

        def scores_of(pair):
            at = columns(pair)
            q = jnp.concatenate(
                [queries[step, other, :, at] for step in steps for other in (0, 1)], axis=0
            )
            q = q * jnp.asarray(HEAD_DIM**-0.5, q.dtype)
            zero = jnp.zeros_like(q)
            q = jnp.concatenate(
                [jnp.where(left, q, zero), jnp.where(left, zero, q)], axis=0
            )
            return lax.dot_general(
                q, keys[:, at], (((1,), (1,)), ((), ())), preferred_element_type=jnp.float32
            )

        def weigh(head, scores):
            cost = costs[pl.ds(head, 1), :]
            old = scores[:, :slots] - cost[:, :slots]
            new = jnp.where(visible, scores[:, slots:] - cost[:, slots:], -DEAD)
            highest = jnp.maximum(
                jnp.max(old, axis=1, keepdims=True), jnp.max(new, axis=1, keepdims=True)
            )
            weights = jnp.concatenate(
                [
                    jnp.exp(old - highest).astype(jnp.bfloat16),
                    jnp.exp(new - highest).astype(jnp.bfloat16),
                ],
                axis=1,
            )
            value_pair = jnp.concatenate(
                [
                    values[:, columns(head // 2)],
                    jnp.ones((all_keys, 2 * HEAD_DIM), values.dtype),
                ],
                axis=1,
            )
            summed = jnp.dot(weights, value_pair, preferred_element_type=jnp.float32)
            sums = summed[:, 2 * HEAD_DIM :]
            return summed[:, : 2 * HEAD_DIM] / sums, highest + jnp.log(sums)

        ahead = scores_of(0)
        for pair in range(pairs):
            at = columns(pair)
            both = []
            for head in (2 * pair, 2 * pair + 1):
                if head == BETWEEN:
                    between()
                if head % 2 == 0:
                    pair_scores = ahead
                    ahead = scores_of(pair + 1) if pair + 1 < pairs else None
                first = head % 2 * chunk
                scores = pair_scores[first : first + chunk]
                mean, log = weigh(head, scores)
                both.append(mean)
                packed = jnp.where(key_lane == head, log, packed)
            out = jnp.where(left, both[0], both[1]).astype(jnp.bfloat16)
            for i in range(2 * span):
                parts_out[steps[i // 2], i % 2, :, at] = out[i * rows : (i + 1) * rows]
        stat = write_logs(packed, heads)
        for i in range(2 * span):
            parts_out[steps[i // 2], i % 2, :, pl.ds(width, PAGE)] = stat[
                i * rows : (i + 1) * rows
            ]
        for step in steps:
            pair_copy(step).start()

    turns = CHIPS // span

    def turn(index, _):
        @pl.when(index > 0)
        def _():
            for step in steps_of(index):
                query_relay(step).wait_recv()

        def between():
            @pl.when(index < turns - 1)
            def _():
                for step in steps_of(index + 1):
                    query_direct(CHIPS - step, 0).wait_recv()
                    query_relay(step).start()

            @pl.when(index > 0)
            def _():
                join_pair(index - 1)

        attend(index, between)
        return 0

    lax.fori_loop(0, turns, turn, 0)
    join_pair(turns - 1)

    for step in range(1, CHIPS):
        part_copy(CHIPS - step).wait_recv()

    def part(step, at):
        return parts_in[step, :, at] if step else merged[0, :, at]

    factors, _ = merge_weights(
        [read_logs(part(step, pl.ds(width, PAGE))) for step in range(CHIPS)], spread[...], heads
    )
    attention = jnp.zeros((rows, width), jnp.float32)
    for step in range(CHIPS):
        attention = attention + factors[step * rows : (step + 1) * rows] * part(
            step, pl.ds(0, width)
        ).astype(jnp.float32)
    attention = attention.astype(jnp.bfloat16)

    def share_copy(step):
        return pltpu.make_async_remote_copy(
            src_ref=shares_out.at[step - 1],
            dst_ref=shares_in.at[tp_count - step - 1],
            send_sem=share_send.at[step - 1],
            recv_sem=share_recv.at[tp_count - step - 1],
            device_id=(seq, (tp + step) % tp_count),
            device_id_type=MESH,
        )

    def share(step):
        block = (tp + step) % tp_count
        columns = pl.ds(pl.multiple_of(block * width, PAGE), width)
        return jnp.dot(attention, weight[:, columns], preferred_element_type=jnp.float32)

    for step in (2, 1, 3)[: tp_count - 1]:
        shares_out[step - 1] = share(step).astype(jnp.bfloat16)
        share_copy(step).start()
    summed = share(0) + residual_ref[...].astype(jnp.float32)
    for step in range(1, tp_count):
        share_copy(step).wait_recv()
        summed = summed + shares_in[tp_count - step - 1].astype(jnp.float32)
    out_ref[...] = summed.astype(out_ref.dtype)

    for step, other in first_sends + later_sends:
        query_direct(step, other).wait_send()
    for step in (1, 3, 4, 5, 6, 7):
        query_relay(step).wait_send()
    for step, other in peers:
        forget_copy(step, other).wait_send()
    for step in range(CHIPS):
        pair_copy(step).wait_send()
        if step:
            part_copy(step).wait_send()
    for step in range(1, tp_count):
        share_copy(step).wait_send()


def shards(
    queries,
    new_keys,
    new_values,
    forget_logit,
    cache_keys,
    cache_values,
    cache_decay,
    slot_page,
    cache_len,
    residual,
    out_weight,
):
    rows, width = queries.shape
    heads = forget_logit.shape[0]
    slots = cache_keys.shape[0]
    tp_count = lax.axis_size("tp")
    vmem = pl.BlockSpec(memory_space=pltpu.VMEM)
    smem = pl.BlockSpec(memory_space=pltpu.SMEM)
    anywhere = pl.BlockSpec(memory_space=pl.ANY)
    dma = pltpu.SemaphoreType.DMA
    half = jnp.bfloat16
    single = jnp.float32
    return pl.pallas_call(
        functools.partial(layer_kernel, tp_count),
        out_shape=(
            jax.ShapeDtypeStruct((rows, width), half),
            jax.ShapeDtypeStruct((heads, rows), single),
        ),
        in_specs=[
            anywhere, anywhere, anywhere, anywhere, anywhere, anywhere, anywhere, smem, smem,
            anywhere, anywhere,
        ],
        out_specs=(vmem, vmem),
        scratch_shapes=[
            pltpu.VMEM((slots + PAGE, width), half),
            pltpu.VMEM((slots + PAGE, width), half),
            pltpu.VMEM(out_weight.shape, half),
            pltpu.VMEM(forget_logit.shape, single),
            pltpu.VMEM(cache_decay.shape, single),
            pltpu.VMEM(residual.shape, half),
            pltpu.VMEM((8, slots + PAGE), single),
            pltpu.VMEM((CHIPS, 2, rows, width), half),
            pltpu.VMEM((8, PAGE), single),
            pltpu.VMEM((1, PAGE), single),
            pltpu.VMEM((CHIPS, 2, 1, PAGE), single),
            pltpu.VMEM((2 * PAGE, width), half),
            pltpu.VMEM((CHIPS, 2, rows, width + PAGE), half),
            pltpu.VMEM((CHIPS, rows, width + PAGE), half),
            pltpu.VMEM((CHIPS, rows, width + PAGE), half),
            pltpu.VMEM((CHIPS, rows, width + PAGE), half),
            pltpu.VMEM((max(tp_count - 1, 1), rows, width), half),
            pltpu.VMEM((max(tp_count - 1, 1), rows, width), half),
            dma((9,)),
            dma((CHIPS, 2)),
            dma((CHIPS, 2)),
            dma((CHIPS, 2)),
            dma((CHIPS, 2)),
            dma((CHIPS,)),
            dma((CHIPS,)),
            dma((CHIPS,)),
            dma((CHIPS,)),
            dma((max(tp_count - 1, 1),)),
            dma((max(tp_count - 1, 1),)),
        ],
        compiler_params=pltpu.CompilerParams(
            collective_id=0, has_side_effects=True, vmem_limit_bytes=60 * 1024 * 1024
        ),
        name="layer",
    )(
        queries, new_keys, new_values, forget_logit, cache_keys, cache_values, cache_decay,
        slot_page, cache_len, residual, out_weight,
    )


def solution(mesh):
    return jax.shard_map(
        shards,
        mesh=mesh,
        in_specs=(
            P("seq", "tp"),
            P("seq", "tp"),
            P("seq", "tp"),
            P("tp", "seq"),
            P("seq", "tp"),
            P("seq", "tp"),
            P("tp", "seq"),
            P("seq"),
            P(),
            P("seq", "tp"),
            P("tp", None),
        ),
        out_specs=(P("seq", "tp"), P("tp", "seq")),
        check_vma=False,
    )
```
